512 devices in a mesh: gx: 8 (over y, core), gy: 16 (over x, z_lo), gz: 4 (over z_hi).
Axes of the slice: x: 4, y: 4, z: 16 (z_hi: 4, z_lo: 4; z = z_hi * 4 + z_lo), core: 2. Of those that a mesh axis runs over, the one named last changes fastest.
Arguments:
- right_side: float32 [8, 16, 4, 64, 512], P('gx', 'gy', 'gz'), may hold values from -6 to 6
- diag_blocks: float32 [4, 64, 64], replicated, may hold values from -0.27 to 17.9, as said below
- face_blocks: float32 [6, 4, 64, 64], replicated, may hold values from -2.42 to 0.22
- prolong: float32 [8, 64, 64], replicated, may hold values from -0.75 to 0.75
- mats_fine: int32 [8, 16, 4, 512], P('gx', 'gy', 'gz'), may hold values from 0 to 3
- mats_mid: int32 [8, 16, 4, 64], P('gx', 'gy', 'gz'), may hold values from 0 to 3
- mats_coarse: int32 [8, 16, 4, 8], P('gx', 'gy', 'gz'), may hold values from 0 to 3
Outputs:
- solution: float32 [8, 16, 4, 64, 512], P('gx', 'gy', 'gz')
The draws below stay inside these ranges and needn't reach their ends.
Inputs may be any that keep to these rules, and one draw needn't show every extreme that they name: `diag_blocks`: each block is symmetric positive definite.
All inputs are finite; a program needn't handle non-finite values.
Results may differ from the reference program's by a relative error of at most 0.0003.
Values sent between devices are 32-bit elements; how exact they have to be, the bound alone decides.
A program may use at most 64 MiB of HBM per device.

```python
import jax
import jax.numpy as jnp
from jax import lax

MODES = 64
MATERIALS = 4
SWEEPS = 2
COARSE_SWEEPS = 4
CYCLES = 2
CX = 8
CY = 8
CZ = 8
N_GX = 8
N_GY = 16
N_GZ = 4


def material_scales(key):
    scale_key = jax.random.fold_in(key, 7)
    first_key, second_key = jax.random.split(scale_key)
    steps = jnp.arange(MATERIALS, dtype=jnp.float32) * (2.0 / (MATERIALS - 1))
    base = jnp.exp2(steps) * jax.random.uniform(first_key, (MATERIALS,), jnp.float32, 0.9, 1.1)
    return jax.random.permutation(second_key, base)


def draw_diag_blocks(key, part):
    scales = material_scales(key)
    noise = jnp.clip(0.03 * jax.random.normal(key, (MATERIALS, MODES, MODES), jnp.float32), -0.06, 0.06)
    symmetric = 0.5 * (noise + jnp.transpose(noise, (0, 2, 1)))
    blocks = 4.0 * jnp.eye(MODES, dtype=jnp.float32)[None] + symmetric
    return blocks * scales[:, None, None]


def draw_face_blocks(key, part):
    scales = material_scales(key)
    face_key = jax.random.fold_in(key, 11)
    noise = jnp.clip(0.025 * jax.random.normal(face_key, (6, MATERIALS, MODES, MODES), jnp.float32), -0.05, 0.05)
    blocks = -0.5 * jnp.eye(MODES, dtype=jnp.float32)[None, None] + noise
    return blocks * scales[None, :, None, None]


def with_ends(drawn, rng, least, top_value):
    place = [jax.random.randint(jax.random.fold_in(rng, axis), (), 0, length) for axis, length in enumerate(drawn.shape)]
    longest = drawn.shape.index(max(drawn.shape))
    next_to = place[:longest] + [(place[longest] + 1) % drawn.shape[longest]] + place[longest + 1:]
    return drawn.at[tuple(place)].set(least).at[tuple(next_to)].set(top_value)


def shard_levels(rng, dims, cuts, low, high):
    loudness, own = 1.0, jax.random.fold_in(rng, 6)
    for dim, shards_of in cuts:
        heights = jnp.exp(jax.random.uniform(jax.random.fold_in(own, dim), (shards_of,), jnp.float32, low / len(cuts), high / len(cuts)))
        loudness = loudness * jnp.repeat(heights, dims[dim] // shards_of).reshape([-1 if axis == dim else 1 for axis in range(len(dims))])
    return loudness


def bell_draw(key, dims, scale, limit, shards=(), kind=jnp.bfloat16):
    values = jax.random.normal(key, dims, jnp.float32) * scale
    if len(shards) > 0:
        values = shard_levels(key, dims, shards, -0.22, 0.18) * values
    return jnp.clip(values, min=-limit, max=limit).astype(kind)


def setup_inputs(seed: int = 0) -> dict:
    seeds = jax.random.split(jax.random.key(seed), 8)
    return {
        "right_side": bell_draw(seeds[0], (N_GX, N_GY, N_GZ, MODES, CX * CY * CZ), 1.0, 6.0, ((0, 8), (1, 16), (2, 4)), jnp.float32),
        "diag_blocks": draw_diag_blocks(jax.random.fold_in(seeds[7], 71), 0),
        "face_blocks": draw_face_blocks(jax.random.fold_in(seeds[7], 71), 0),
        "prolong": bell_draw(seeds[3], (8, MODES, MODES), MODES ** -0.5, 0.75, (), jnp.float32),
        "mats_fine": with_ends(jax.random.randint(seeds[4], (N_GX, N_GY, N_GZ, CX * CY * CZ), 0, MATERIALS), jax.random.fold_in(seeds[4], 1), 0, MATERIALS - 1).astype(jnp.int32),
        "mats_mid": with_ends(jax.random.randint(seeds[5], (N_GX, N_GY, N_GZ, (CX // 2) * (CY // 2) * (CZ // 2)), 0, MATERIALS), jax.random.fold_in(seeds[5], 1), 0, MATERIALS - 1).astype(jnp.int32),
        "mats_coarse": with_ends(jax.random.randint(seeds[6], (N_GX, N_GY, N_GZ, (CX // 4) * (CY // 4) * (CZ // 4)), 0, MATERIALS), jax.random.fold_in(seeds[6], 1), 0, MATERIALS - 1).astype(jnp.int32),
    }


relax_weight = 0.7
restrict_scale = 0.6
highest = lax.Precision.HIGHEST

def inverse_blocks(diag_blocks):
    identity = jnp.eye(MODES, dtype=diag_blocks.dtype)
    result = []
    for material in range(MATERIALS):
        factor = jnp.linalg.cholesky(diag_blocks[material])
        result.append(jax.scipy.linalg.cho_solve((factor, True), identity))
    return jnp.stack(result).reshape(MATERIALS * MODES, MODES)

def coupling_matrix(diag_blocks, face_blocks):
    blocks = jnp.concatenate([diag_blocks[None], face_blocks], axis=0)
    return jnp.transpose(blocks, (1, 2, 0, 3)).reshape(MATERIALS * MODES, 7 * MODES)

def choose_blocks(weights, columns, onehot):
    product = jnp.dot(weights.astype(jnp.float32), columns.astype(jnp.float32), precision=highest, preferred_element_type=jnp.float32)
    product = product.reshape(MATERIALS, MODES, columns.shape[1])
    return jnp.sum(product * onehot.reshape(MATERIALS, 1, columns.shape[1]), axis=0)

def operate(padded, onehot, coupling):
    centre = padded[:, 1:-1, 1:-1, 1:-1]
    stacked = jnp.concatenate([centre, padded[:, 2:, 1:-1, 1:-1], padded[:, :-2, 1:-1, 1:-1], padded[:, 1:-1, 2:, 1:-1], padded[:, 1:-1, :-2, 1:-1], padded[:, 1:-1, 1:-1, 2:], padded[:, 1:-1, 1:-1, :-2]], axis=0)
    columns = stacked.reshape(7 * MODES, -1)
    return choose_blocks(coupling, columns, onehot.reshape(MATERIALS, -1)).reshape(centre.shape)

def apply_inverse(inverse, field, onehot):
    return choose_blocks(inverse, field.reshape(MODES, -1), onehot.reshape(MATERIALS, -1)).reshape(field.shape)

def zero_border(field):
    return jnp.pad(field, ((0, 0), (1, 1), (1, 1), (1, 1)))

def relax(iterate, source, onehot, inverse, coupling):
    residual = source - operate(zero_border(iterate), onehot, coupling)
    return iterate + relax_weight * apply_inverse(inverse, residual, onehot)

def restrict(field, prolong):
    blocked = field.reshape(MODES, field.shape[1] // 2, 2, field.shape[2] // 2, 2, field.shape[3] // 2, 2)
    return restrict_scale * jnp.einsum('abcji,jxaybzc->ixyz', prolong.reshape(2, 2, 2, MODES, MODES), blocked, precision=highest)

def expand(coarse_field, prolong):
    finer = jnp.einsum('abcji,ixyz->jxaybzc', prolong.reshape(2, 2, 2, MODES, MODES), coarse_field, precision=highest)
    return finer.reshape(MODES, 2 * coarse_field.shape[1], 2 * coarse_field.shape[2], 2 * coarse_field.shape[3])

def to_grid(field, size_x, size_y, size_z):
    blocked = field.reshape(N_GX, N_GY, N_GZ, MODES, size_x, size_y, size_z)
    return jnp.transpose(blocked, (3, 0, 4, 1, 5, 2, 6)).reshape(MODES, N_GX * size_x, N_GY * size_y, N_GZ * size_z)

def onehot_grid(materials, size_x, size_y, size_z):
    blocked = materials.reshape(N_GX, N_GY, N_GZ, size_x, size_y, size_z)
    grid = jnp.transpose(blocked, (0, 3, 1, 4, 2, 5)).reshape(N_GX * size_x, N_GY * size_y, N_GZ * size_z)
    return (grid[None] == jnp.arange(MATERIALS, dtype=jnp.int32)[:, None, None, None]).astype(jnp.float32)

def reference(right_side, diag_blocks, face_blocks, prolong, mats_fine, mats_mid, mats_coarse):
    inverse = inverse_blocks(diag_blocks)
    coupling = coupling_matrix(diag_blocks, face_blocks)
    source = to_grid(right_side, CX, CY, CZ)
    onehot_fine = onehot_grid(mats_fine, CX, CY, CZ)
    onehot_mid = onehot_grid(mats_mid, CX // 2, CY // 2, CZ // 2)
    onehot_coarse = onehot_grid(mats_coarse, CX // 4, CY // 4, CZ // 4)

    def coarse_solve(coarse_source):
        iterate = relax_weight * apply_inverse(inverse, coarse_source, onehot_coarse)
        for repeat in range(COARSE_SWEEPS - 1):
            iterate = relax(iterate, coarse_source, onehot_coarse, inverse, coupling)
        return iterate

    def middle(mid_source):
        iterate = relax_weight * apply_inverse(inverse, mid_source, onehot_mid)
        for repeat in range(SWEEPS - 1):
            iterate = relax(iterate, mid_source, onehot_mid, inverse, coupling)
        residual = mid_source - operate(zero_border(iterate), onehot_mid, coupling)
        iterate = iterate + expand(coarse_solve(restrict(residual, prolong)), prolong)
        for repeat in range(SWEEPS):
            iterate = relax(iterate, mid_source, onehot_mid, inverse, coupling)
        return iterate
    iterate = relax_weight * apply_inverse(inverse, source, onehot_fine)
    for repeat in range(SWEEPS - 1):
        iterate = relax(iterate, source, onehot_fine, inverse, coupling)
    for cycle_index in range(CYCLES):
        if cycle_index > 0:
            for repeat in range(SWEEPS):
                iterate = relax(iterate, source, onehot_fine, inverse, coupling)
        residual = source - operate(zero_border(iterate), onehot_fine, coupling)
        iterate = iterate + expand(middle(restrict(residual, prolong)), prolong)
        for repeat in range(SWEEPS):
            iterate = relax(iterate, source, onehot_fine, inverse, coupling)
    blocked = iterate.reshape(MODES, N_GX, CX, N_GY, CY, N_GZ, CZ)
    return jnp.transpose(blocked, (1, 3, 5, 0, 2, 4, 6)).reshape(N_GX, N_GY, N_GZ, MODES, CX * CY * CZ)
```

```python
from functools import partial

import jax
import jax.numpy as jnp
from jax import lax
from jax.experimental import pallas as pl
from jax.experimental.pallas import tpu as pltpu
from jax.sharding import PartitionSpec as P

MODES = 64
MATERIALS = 4
SWEEPS = 2
COARSE_SWEEPS = 4
CYCLES = 2
ROWS = (512, 64, 8)
TILE_DIMS = ((2, 2, 2, 2, 2, 2), (2, 2, 2), ())
FACE_ROWS = (32, 8, 8)
AXES = ("gx", "gy", "gz")
WEIGHT = 0.7
SCALE = 0.6
SUB = (4, 2, 1)
f32 = jnp.float32
bf16 = jnp.bfloat16
highest = lax.Precision.HIGHEST


def lanes(rows):
    return lax.broadcasted_iota(jnp.int32, (rows, 128), 1)


def swap_halves(x):
    return pltpu.roll(x, 64, axis=1)


def split(x):
    high = x.astype(bf16).astype(f32)
    return jnp.where(lanes(x.shape[0]) < 64, high, x - high)


def bit_is(dim, value):
    sub = lax.broadcasted_iota(jnp.int32, (8, 128), 0)
    return (jnp.right_shift(sub, 2 - dim) & 1) == value


def roll_sub(x, amount):
    shape = x.shape
    return pltpu.roll(x.reshape(-1, 8, 128), (-amount) % 8, axis=1).reshape(shape)


def pair(weights):
    high = weights.astype(bf16)
    return high, (weights - high.astype(f32)).astype(bf16)


def chosen(product, material):
    rows = product.shape[0]
    half = jnp.where(lanes(rows) < 64, 0.0, 1.0)
    offset = material - half
    kept = jnp.where(offset == 0.0, product[:, :128], jnp.where(offset == 2.0, product[:, 128:], 0.0))
    return kept + swap_halves(kept)


def twice(x, w_ref):
    return jnp.dot(jnp.concatenate([x, x], axis=1), w_ref[...], preferred_element_type=f32)


def three(x):
    a = x.astype(bf16)
    rest = x - a.astype(f32)
    b = rest.astype(bf16)
    return a, b, (rest - b.astype(f32)).astype(bf16)


def element_of_row(row):
    def bit(n):
        return jnp.right_shift(row, n) & 1
    x = bit(8) + 2 * bit(5) + 4 * bit(2)
    y = bit(7) + 2 * bit(4) + 4 * bit(1)
    z = bit(6) + 2 * bit(3) + 4 * bit(0)
    return x * 64 + y * 8 + z


def middle_of_row(row):
    def bit(n):
        return jnp.right_shift(row, n) & 1
    x = bit(5) + 2 * bit(2)
    y = bit(4) + 2 * bit(1)
    z = bit(3) + 2 * bit(0)
    return x * 16 + y * 4 + z


def spread_materials(mats, rows, place):
    row = lax.broadcasted_iota(jnp.int32, (rows, rows), 0)
    col = lax.broadcasted_iota(jnp.int32, (rows, rows), 1)
    kept = jnp.where(place(row) == col, jnp.broadcast_to(mats.astype(f32), (rows, rows)), 0.0)
    return jnp.broadcast_to(jnp.sum(kept, axis=1, keepdims=True), (rows, 128))


def invert(blocks):
    row_id = lax.broadcasted_iota(jnp.int32, blocks.shape, 1)
    lane_id = lax.broadcasted_iota(jnp.int32, blocks.shape, 2)
    for k in range(MODES):
        pivot = 1.0 / blocks[:, k:k + 1, k:k + 1]
        at_lane = lane_id == k
        row = jnp.where(at_lane[:, :1, :], 1.0, blocks[:, k:k + 1, :]) * pivot
        column = blocks[:, :, k:k + 1]
        rest = jnp.where(at_lane, 0.0, blocks) - column * row
        blocks = jnp.where(row_id == k, row, rest)
    return blocks


def prepare(diag_ref, face_ref, prolong_ref, sweep_w, rest_w, inv_w, restrict_w, prolong_w):
    inverse = invert(diag_ref[...])

    def side(parts):
        return jnp.concatenate(parts, axis=1)

    def store(ref, at, w):
        high, low = pair(w)
        half = ref.shape[0] // 2
        ref[at:at + 128] = jnp.concatenate([high, high], axis=0)
        ref[half + at:half + at + 128] = jnp.concatenate([low, low], axis=0)
    store(inv_w, 0, WEIGHT * side([inverse[m] for m in range(MATERIALS)]))
    store(rest_w, 6 * 128, side([diag_ref[m] for m in range(MATERIALS)]))
    for d in range(6):
        turned = [jnp.transpose(face_ref[d, m]) for m in range(MATERIALS)]
        store(rest_w, d * 128, side(turned))
        mixed = [
            jnp.dot(turned[m], inverse[m], precision=highest, preferred_element_type=f32)
            for m in range(MATERIALS)
        ]
        store(sweep_w, d * 128, -WEIGHT * side(mixed))
    for c in range(8):
        block = SCALE * prolong_ref[c]
        store(restrict_w, c * 128, side([block, block]))
        back = jnp.transpose(prolong_ref[c])
        high, low = pair(side([back, back]))
        columns = slice(c * 128, c * 128 + 128)
        prolong_w[0:128, columns] = jnp.concatenate([high, high], axis=0)
        prolong_w[128:256, columns] = jnp.concatenate([low, low], axis=0)


def index_at(level, dim, *bits):
    at = [slice(None)] * len(TILE_DIMS[level])
    for i, b in enumerate(bits):
        at[3 * i + dim] = b
    return tuple(at)


def depth(level):
    return 2 - level


def face_tiles(value, level, dim, upper):
    tiles = value.reshape(TILE_DIMS[level] + (8, 128))
    return tiles[index_at(level, dim, *([1 if upper else 0] * depth(level)))].reshape(-1, 8, 128)


def pack_face(value, level, dim, upper):
    tiles = face_tiles(value, level, dim, upper)
    target = 0 if upper else 1
    amount = SUB[dim] if upper else -SUB[dim]
    count = tiles.shape[0]
    if count == 1:
        return roll_sub(tiles, amount).reshape(8, 128)
    half = count // 2
    packed = jnp.where(bit_is(dim, target), roll_sub(tiles[:half], amount), tiles[half:])
    half = half // 2
    packed = jnp.where(lanes(8) < 64, packed[:half], packed[half:])
    return packed.reshape(-1, 128)


def unpack_face(packed, level, dim, from_upper):
    amount = -SUB[dim] if from_upper else SUB[dim]
    if level == 2:
        return split(packed).reshape(1, 8, 128)
    other = swap_halves(packed)
    low_lanes = lanes(packed.shape[0]) < 64
    both = jnp.concatenate([jnp.where(low_lanes, packed, other), jnp.where(low_lanes, other, packed)], axis=0)
    both = split(both).reshape(-1, 8, 128)
    return jnp.concatenate([both, roll_sub(both, amount)], axis=0)


def border(tiles, halo, dim, up):
    rolled = roll_sub(tiles, SUB[dim] if up else -SUB[dim])
    return jnp.where(bit_is(dim, 0 if up else 1), rolled, halo.reshape(tiles.shape))


def place_inner(lhs, u, d):
    dim, up = d // 2, d % 2 == 0
    tiles = u.reshape(TILE_DIMS[0] + (8, 128))
    near, far = (0, 1) if up else (1, 0)

    def put(where, value):
        shape = value.shape[:-3] + (16, 128)
        lhs[(d,) + where] = value.reshape(shape).astype(bf16)
    put(index_at(0, dim, near)[:5], tiles[index_at(0, dim, far)])
    if dim < 2:
        put(index_at(0, dim, far, near)[:5], tiles[index_at(0, dim, near, far)])


def place_border(lhs, u, d, halo):
    dim, up = d // 2, d % 2 == 0
    tiles = u.reshape(TILE_DIMS[0] + (8, 128))
    near, far = (0, 1) if up else (1, 0)
    edge = border(tiles[index_at(0, dim, near, near)], halo, dim, up)
    if dim < 2:
        lhs[(d,) + index_at(0, dim, far, far)[:5]] = edge.reshape(edge.shape[:-3] + (16, 128)).astype(bf16)
    else:
        inner = tiles[index_at(0, dim, near, far)]
        both = [inner, edge] if up else [edge, inner]
        both = jnp.concatenate(both, axis=-2)
        lhs[d, :, :, far] = both.astype(bf16)


def shifted(u, level, d, halo):
    dim, up = d // 2, d % 2 == 0
    if level == 2:
        return border(u.reshape(1, 8, 128), halo, dim, up).reshape(8, 128)
    tiles = u.reshape(TILE_DIMS[1] + (8, 128))
    first = tiles[index_at(1, dim, 1 if up else 0)]
    edge = border(tiles[index_at(1, dim, 0 if up else 1)], halo, dim, up)
    parts = [first, edge] if up else [edge, first]
    return jnp.stack(parts, axis=dim).reshape(64, 128)


def kernel(
    sizes, rhs_ref, diag_ref, face_ref, prolong_ref, fine_ref, mid_ref, coarse_ref, out_ref,
    sweep_w, rest_w, inv_w, restrict_w, prolong_w, order, lhs,
    v0, f0, g0, m0, v1, f1, g1, m1, v2, g2, m2, out_box, in_box, send_sem, recv_sem,
):
    place = [lax.axis_index(axis) for axis in AXES]
    sides = []
    for d in range(6):
        dim, up = d // 2, d % 2 == 0
        there = list(place)
        there[dim] = place[dim] + (1 if up else -1)
        exists = (place[dim] < sizes[dim] - 1) if up else (place[dim] > 0)
        sides.append((exists, tuple(there)))

    barrier = pltpu.get_barrier_semaphore()
    for exists, there in sides:
        @pl.when(exists)
        def _():
            pl.semaphore_signal(barrier, inc=1, device_id=there, device_id_type=pl.DeviceIdType.MESH)
    pl.semaphore_wait(barrier, sum(exists.astype(jnp.int32) for exists, there in sides))
    for d, (exists, there) in enumerate(sides):
        @pl.when(jnp.logical_not(exists))
        def _():
            in_box[:, d] = jnp.zeros((2, 32, 128), f32)

    prepare(diag_ref, face_ref, prolong_ref, sweep_w, rest_w, inv_w, restrict_w, prolong_w)
    row = lax.broadcasted_iota(jnp.int32, (512, 512), 0)
    col = lax.broadcasted_iota(jnp.int32, (512, 512), 1)
    order[...] = jnp.where(element_of_row(row) == col, 1.0, 0.0).astype(bf16)
    m0[...] = lax.dot_general(
        order[...], jnp.broadcast_to(fine_ref[...].astype(f32), (128, 512)).astype(bf16),
        (((1,), (1,)), ((), ())), preferred_element_type=f32)
    m1[...] = spread_materials(mid_ref[...], 64, middle_of_row)
    m2[...] = spread_materials(coarse_ref[...], 8, lambda r: r)
    source = jnp.concatenate([rhs_ref[...], rhs_ref[...]], axis=0)
    total = None
    for piece in three(source):
        part = lax.dot_general(order[...], piece, (((1,), (1,)), ((), ())), preferred_element_type=f32)
        total = part if total is None else total + part
    f0[...] = total

    def scaled_inverse(value, material):
        return chosen(twice(split(value).astype(bf16), inv_w), material)

    g0[...] = scaled_inverse(f0[...], m0[...])
    v0[...] = g0[...]
    state = ((v0, g0, m0), (v1, g1, m1), (v2, g2, m2))

    def copy_of(d, level, slot):
        rows = pl.ds(0, FACE_ROWS[level])
        return pltpu.make_async_remote_copy(
            src_ref=out_box.at[slot, d, rows],
            dst_ref=in_box.at[slot, d ^ 1, rows],
            send_sem=send_sem.at[slot, d],
            recv_sem=recv_sem.at[slot, d ^ 1],
            device_id=sides[d][1],
            device_id_type=pl.DeviceIdType.MESH,
        )

    def arrival_of(d, level, slot):
        rows = pl.ds(0, FACE_ROWS[level])
        return pltpu.make_async_remote_copy(
            src_ref=out_box.at[slot, d, rows],
            dst_ref=in_box.at[slot, d, rows],
            send_sem=send_sem.at[slot, d],
            recv_sem=recv_sem.at[slot, d],
            device_id=sides[d][1],
            device_id_type=pl.DeviceIdType.MESH,
        )

    def gathered(level, step):
        slot = lax.rem(step, 2)
        value = state[level][0][...]
        for d in (4, 5, 2, 3, 0, 1):
            out_box[slot, d, :FACE_ROWS[level]] = pack_face(value, level, d // 2, d % 2 == 0)
        for d in (4, 5, 2, 3, 0, 1):
            @pl.when(sides[d][0])
            def _():
                copy_of(d, level, slot).start()
        u = split(value)
        if level == 0:
            for d in range(6):
                place_inner(lhs, u, d)
            lhs[6] = u.reshape(2, 2, 2, 2, 2, 16, 128).astype(bf16)
        for d in range(6):
            @pl.when(sides[d][0])
            def _():
                arrival_of(d, level, slot).wait_recv()
        fields = []
        for d in range(6):
            halo = unpack_face(in_box[slot, d, :FACE_ROWS[level]], level, d // 2, d % 2 == 0)
            if level == 0:
                place_border(lhs, u, d, halo)
            else:
                fields.append(shifted(u, level, d, halo))
        for d in range(6):
            @pl.when(sides[d][0])
            def _():
                copy_of(d, level, slot).wait_send()
        if level == 0:
            return [lhs[d].reshape(512, 128) for d in range(7)]
        fields.append(u)
        if level == 2:
            fields = [jnp.concatenate([field, field], axis=0) for field in fields]
        return [field.astype(bf16) for field in fields]

    def sweep(level, step):
        v, g, m = state[level]
        product = twice(jnp.concatenate(gathered(level, step)[:6], axis=1), sweep_w)
        v[...] = (1.0 - WEIGHT) * v[...] + g[...] + chosen(product[:ROWS[level]], m[...])

    def residual(level, step):
        f = (f0, f1)[level]
        product = twice(jnp.concatenate(gathered(level, step), axis=1), rest_w)
        return f[...] - chosen(product, state[level][2][...])

    def coarser(value):
        u = split(value)
        count = u.shape[0] // 8
        parts = [u[c * count:(c + 1) * count] for c in range(8)]
        if count == 8:
            parts = [jnp.concatenate([part, part], axis=0) for part in parts]
        return twice(jnp.concatenate(parts, axis=1).astype(bf16), restrict_w)[:count]

    def finer(value):
        u = split(value)
        count = u.shape[0]
        if count == 8:
            u = jnp.concatenate([u, u], axis=0)
        product = twice(u.astype(bf16), prolong_w)[:count]
        return jnp.concatenate([product[:, c * 128:(c + 1) * 128] for c in range(8)], axis=0)

    def wide(value):
        return jnp.concatenate([value, value], axis=0)

    @pl.loop(0, CYCLES)
    def _(cycle):
        base = 11 * cycle

        @pl.loop(0, SWEEPS - 1 + cycle)
        def _(i):
            sweep(0, base + i)
        f1[...] = coarser(residual(0, base + SWEEPS - 1 + cycle))
        base = base + SWEEPS + cycle
        g1[...] = scaled_inverse(f1[...], m1[...])
        v1[...] = g1[...]
        for i in range(SWEEPS - 1):
            sweep(1, base + i)
        base = base + SWEEPS - 1
        f2 = coarser(residual(1, base))
        base = base + 1
        g2[...] = scaled_inverse(wide(f2), wide(m2[...]))[:8]
        v2[...] = g2[...]

        @pl.loop(0, COARSE_SWEEPS - 1)
        def _(i):
            sweep(2, base + i)
        base = base + COARSE_SWEEPS - 1
        v1[...] = v1[...] + finer(v2[...])

        @pl.loop(0, SWEEPS)
        def _(i):
            sweep(1, base + i)
        base = base + SWEEPS
        v0[...] = v0[...] + finer(v1[...])

        @pl.loop(0, SWEEPS)
        def _(i):
            sweep(0, base + i)

    result = jnp.transpose(v0[...])[:MODES]
    total = None
    for piece in three(result):
        part = jnp.dot(piece, order[...], preferred_element_type=f32)
        total = part if total is None else total + part
    out_ref[...] = total


def per_device(sizes, right_side, diag_blocks, face_blocks, prolong, mats_fine, mats_mid, mats_coarse):
    def vmem(shape, dtype=f32):
        return pltpu.VMEM(shape, dtype)
    field = [vmem((512, 128))] * 4
    middle = [vmem((64, 128))] * 4
    coarse = [vmem((8, 128))] * 3
    result = pl.pallas_call(
        partial(kernel, sizes),
        out_shape=jax.ShapeDtypeStruct((MODES, 512), f32),
        in_specs=[pl.BlockSpec(memory_space=pltpu.VMEM)] * 7,
        out_specs=pl.BlockSpec(memory_space=pltpu.VMEM),
        scratch_shapes=[
            vmem((2 * 768, 256), bf16),
            vmem((2 * 896, 256), bf16),
            vmem((2 * 128, 256), bf16),
            vmem((2 * 1024, 128), bf16),
            vmem((2 * 128, 1024), bf16),
            vmem((512, 512), bf16),
            vmem((7, 2, 2, 2, 2, 2, 16, 128), bf16),
        ] + field + middle + coarse + [
            vmem((2, 6, 32, 128)),
            vmem((2, 6, 32, 128)),
            pltpu.SemaphoreType.DMA((2, 6)),
            pltpu.SemaphoreType.DMA((2, 6)),
        ],
        compiler_params=pltpu.CompilerParams(collective_id=0, has_side_effects=True),
        name="cycles",
    )(
        right_side[0, 0, 0], diag_blocks, face_blocks, prolong,
        mats_fine.reshape(1, -1), mats_mid.reshape(1, -1), mats_coarse.reshape(1, -1),
    )
    return result[None, None, None]


def solution(mesh):
    placed = (
        P("gx", "gy", "gz", None, None),
        P(),
        P(),
        P(),
        P("gx", "gy", "gz", None),
        P("gx", "gy", "gz", None),
        P("gx", "gy", "gz", None),
    )
    sizes = tuple(mesh.shape[axis] for axis in AXES)
    return jax.shard_map(
        partial(per_device, sizes),
        mesh=mesh,
        in_specs=placed,
        out_specs=P("gx", "gy", "gz", None, None),
        check_vma=False,
    )
```

```python
from functools import partial

import jax
import jax.numpy as jnp
from jax import lax
from jax.experimental import pallas as pl
from jax.experimental.pallas import tpu as pltpu
from jax.sharding import PartitionSpec as P

MODES = 64
MATERIALS = 4
SWEEPS = 2
COARSE_SWEEPS = 4
CYCLES = 2
ROWS = (512, 64, 8)
TILE_DIMS = ((2, 2, 2, 2, 2, 2), (2, 2, 2), ())
FACE_ROWS = (32, 8, 8)
AXES = ("gx", "gy", "gz")
WEIGHT = 0.7
SCALE = 0.6
SUB = (4, 2, 1)
f32 = jnp.float32
bf16 = jnp.bfloat16
highest = lax.Precision.HIGHEST


def lanes(rows):
    return lax.broadcasted_iota(jnp.int32, (rows, 128), 1)


def swap_halves(x):
    return pltpu.roll(x, 64, axis=1)


def split(x):
    high = x.astype(bf16).astype(f32)
    return jnp.where(lanes(x.shape[0]) < 64, high, x - high)


def bit_is(dim, value):
    sub = lax.broadcasted_iota(jnp.int32, (8, 128), 0)
    return (jnp.right_shift(sub, 2 - dim) & 1) == value


def roll_sub(x, amount):
    shape = x.shape
    return pltpu.roll(x.reshape(-1, 8, 128), (-amount) % 8, axis=1).reshape(shape)


def pair(weights):
    high = weights.astype(bf16)
    return high, (weights - high.astype(f32)).astype(bf16)


def chosen(product, material):
    rows = product.shape[0]
    half = jnp.where(lanes(rows) < 64, 0.0, 1.0)
    offset = material - half
    kept = jnp.where(offset == 0.0, product[:, :128], jnp.where(offset == 2.0, product[:, 128:], 0.0))
    return kept + swap_halves(kept)


def twice(x, w_ref):
    return jnp.dot(jnp.concatenate([x, x], axis=1), w_ref[...], preferred_element_type=f32)


def three(x):
    a = x.astype(bf16)
    rest = x - a.astype(f32)
    b = rest.astype(bf16)
    return a, b, (rest - b.astype(f32)).astype(bf16)


def element_of_row(row):
    def bit(n):
        return jnp.right_shift(row, n) & 1
    x = bit(8) + 2 * bit(5) + 4 * bit(2)
    y = bit(7) + 2 * bit(4) + 4 * bit(1)
    z = bit(6) + 2 * bit(3) + 4 * bit(0)
    return x * 64 + y * 8 + z


def middle_of_row(row):
    def bit(n):
        return jnp.right_shift(row, n) & 1
    x = bit(5) + 2 * bit(2)
    y = bit(4) + 2 * bit(1)
    z = bit(3) + 2 * bit(0)
    return x * 16 + y * 4 + z


def spread_materials(mats, rows, place):
    row = lax.broadcasted_iota(jnp.int32, (rows, rows), 0)
    col = lax.broadcasted_iota(jnp.int32, (rows, rows), 1)
    kept = jnp.where(place(row) == col, jnp.broadcast_to(mats.astype(f32), (rows, rows)), 0.0)
    return jnp.broadcast_to(jnp.sum(kept, axis=1, keepdims=True), (rows, 128))


def invert(blocks):
    row_id = lax.broadcasted_iota(jnp.int32, blocks.shape, 1)
    lane_id = lax.broadcasted_iota(jnp.int32, blocks.shape, 2)
    for k in range(MODES):
        pivot = 1.0 / blocks[:, k:k + 1, k:k + 1]
        at_lane = lane_id == k
        row = jnp.where(at_lane[:, :1, :], 1.0, blocks[:, k:k + 1, :]) * pivot
        column = blocks[:, :, k:k + 1]
        rest = jnp.where(at_lane, 0.0, blocks) - column * row
        blocks = jnp.where(row_id == k, row, rest)
    return blocks


def prepare(diag_ref, face_ref, prolong_ref, sweep_w, rest_w, inv_w, restrict_w, prolong_w):
    inverse = invert(diag_ref[...])

    def side(parts):
        return jnp.concatenate(parts, axis=1)

    def store(ref, at, w):
        high, low = pair(w)
        half = ref.shape[0] // 2
        ref[at:at + 128] = jnp.concatenate([high, high], axis=0)
        ref[half + at:half + at + 128] = jnp.concatenate([low, low], axis=0)
    store(inv_w, 0, WEIGHT * side([inverse[m] for m in range(MATERIALS)]))
    store(rest_w, 6 * 128, side([diag_ref[m] for m in range(MATERIALS)]))
    for d in range(6):
        turned = [jnp.transpose(face_ref[d, m]) for m in range(MATERIALS)]
        store(rest_w, d * 128, side(turned))
        mixed = [
            jnp.dot(turned[m], inverse[m], precision=highest, preferred_element_type=f32)
            for m in range(MATERIALS)
        ]
        store(sweep_w, d * 128, -WEIGHT * side(mixed))
    for c in range(8):
        block = SCALE * prolong_ref[c]
        store(restrict_w, c * 128, side([block, block]))
        back = jnp.transpose(prolong_ref[c])
        high, low = pair(side([back, back]))
        columns = slice(c * 128, c * 128 + 128)
        prolong_w[0:128, columns] = jnp.concatenate([high, high], axis=0)
        prolong_w[128:256, columns] = jnp.concatenate([low, low], axis=0)


def index_at(level, dim, *bits):
    at = [slice(None)] * len(TILE_DIMS[level])
    for i, b in enumerate(bits):
        at[3 * i + dim] = b
    return tuple(at)


def depth(level):
    return 2 - level


PAIRS = ((0, 1), (0, 2), (1, 2))
EDGES = tuple((p, q, sp, sq) for p, q in PAIRS for sp in (0, 1) for sq in (0, 1))
SLOTS = 3


def own_tiles(value, level):
    return value.reshape(TILE_DIMS[level] + (8, 128))


def outer(tiles, level, dim, upper, layer):
    bits = [upper] * depth(level)
    if layer == 2 and bits:
        bits[0] = 1 - upper
    return tiles[index_at(level, dim, *bits)].reshape(-1, 8, 128)


def toward(dim, upper):
    return SUB[dim] if upper else -SUB[dim]


def two_halves(packed):
    other = swap_halves(packed.reshape(-1, 128)).reshape(packed.shape)
    low_lanes = lanes(8) < 64
    return jnp.concatenate([jnp.where(low_lanes, packed, other), jnp.where(low_lanes, other, packed)], axis=0)


def pack_face(tiles, level, dim, upper, layer):
    tiles = outer(tiles, level, dim, upper, layer)
    half = tiles.shape[0] // 2
    packed = jnp.where(bit_is(dim, 1 - upper), roll_sub(tiles[:half], toward(dim, upper)), tiles[half:])
    half = half // 2
    return jnp.where(lanes(8) < 64, packed[:half], packed[half:]).reshape(-1, 128)


def unpack_face(packed, level, dim, upper, layer):
    packed = packed.reshape(-1, 8, 128)
    if level == 2:
        return packed if layer == 2 else roll_sub(packed, -toward(dim, upper))
    both = two_halves(packed)
    return jnp.concatenate([both, roll_sub(both, -toward(dim, upper))], axis=0)


def pack_edge(tiles, level, p, q, sp, sq):
    at = list(index_at(level, p, *([sp] * depth(level))))
    for i, b in enumerate(index_at(level, q, *([sq] * depth(level)))):
        at[i] = b if at[i] == slice(None) else at[i]
    tiles = tiles[tuple(at)].reshape(-1, 8, 128)
    half = tiles.shape[0] // 2
    if level == 0:
        moved = roll_sub(tiles[:half], toward(p, sp) + toward(q, sq))
        tiles = jnp.where(bit_is(p, 1 - sp), moved, roll_sub(tiles[half:], toward(q, sq)))
    else:
        tiles = roll_sub(tiles, toward(p, sp) + toward(q, sq))
    return jnp.where(lanes(8) < 64, tiles[0], tiles[1])


def unpack_edge(packed, level, p, q, sp, sq):
    packed = packed.reshape(1, 8, 128)
    if level == 2:
        return roll_sub(packed, -toward(p, sp) - toward(q, sq))
    both = two_halves(packed)
    if level == 1:
        return both
    return jnp.concatenate([both, roll_sub(both, -toward(p, sp))], axis=0)


def split_tiles(tiles):
    return split(tiles.reshape(-1, 128)).reshape(tiles.shape)


def border(tiles, halo, dim, up):
    rolled = roll_sub(tiles, SUB[dim] if up else -SUB[dim])
    return jnp.where(bit_is(dim, 0 if up else 1), rolled, halo.reshape(tiles.shape))


def take(tiles, axis, bit):
    at = [slice(None)] * tiles.ndim
    at[axis] = bit
    return tiles[tuple(at)]


def shifted(tiles, axes, dim, up, halo):
    if not axes:
        return border(tiles, halo, dim, up)
    near, far = (0, 1) if up else (1, 0)

    def ordered(at_near, at_far, axis):
        return jnp.stack([at_near, at_far] if up else [at_far, at_near], axis=axis)
    if len(axes) == 1:
        return ordered(take(tiles, axes[0], far), border(take(tiles, axes[0], near), halo, dim, up), axes[0])
    kept = take(tiles, axes[0], near)
    deeper = axes[1] - 1
    end = border(take(kept, deeper, near), halo, dim, up)
    return ordered(take(tiles, axes[0], far), ordered(take(kept, deeper, far), end, deeper), axes[0])


def place_inner(lhs, u, d):
    dim, up = d // 2, d % 2 == 0
    tiles = own_tiles(u, 0)
    near, far = (0, 1) if up else (1, 0)

    def put(where, value):
        shape = value.shape[:-3] + (16, 128)
        lhs[(d,) + where] = value.reshape(shape).astype(bf16)
    put(index_at(0, dim, near)[:5], tiles[index_at(0, dim, far)])
    if dim < 2:
        put(index_at(0, dim, far, near)[:5], tiles[index_at(0, dim, near, far)])


def place_border(lhs, u, d, halo):
    dim, up = d // 2, d % 2 == 0
    tiles = own_tiles(u, 0)
    near, far = (0, 1) if up else (1, 0)
    edge = border(tiles[index_at(0, dim, near, near)], halo, dim, up)
    if dim < 2:
        lhs[(d,) + index_at(0, dim, far, far)[:5]] = edge.reshape(edge.shape[:-3] + (16, 128)).astype(bf16)
    else:
        inner = tiles[index_at(0, dim, near, far)]
        both = [inner, edge] if up else [edge, inner]
        both = jnp.concatenate(both, axis=-2)
        lhs[d, :, :, far] = both.astype(bf16)


def halo_fields(u, level, dim, near, far, edges):
    tiles = own_tiles(u, level)
    others = [i for i in range(3) if i != dim]
    bits = near.reshape((2,) * (2 * depth(level)) + (8, 128))
    fields = []
    for d in range(6):
        along, up = d // 2, d % 2 == 0
        if along == dim:
            own = outer(tiles, level, dim, 0 if up else 1, 1)
            field = jnp.where(bit_is(dim, 1 if up else 0), far, own)
        else:
            axes = [others.index(along) + 2 * i for i in range(depth(level))]
            field = shifted(bits, axes, along, up, edges[PAIRS.index((min(dim, along), max(dim, along)))])
        fields.append(field.reshape(-1, 128))
    return jnp.concatenate(fields, axis=1)


def kernel(
    sizes, rhs_ref, diag_ref, face_ref, prolong_ref, fine_ref, mid_ref, coarse_ref, out_ref,
    sweep_w, rest_w, inv_w, restrict_w, prolong_w, order, lhs,
    v0, f0, g0, m0, v1, f1, g1, m1, v2, g2, m2,
    halo_g0, halo_g1, halo_g2, halo_m0, halo_m1, halo_m2,
    out_face, in_face, out_edge, in_edge, out_mat, in_mat,
    send_face, recv_face, send_edge, recv_edge, send_mat, recv_mat,
):
    place = [lax.axis_index(axis) for axis in AXES]
    able = [((place[i] > 0), (place[i] < sizes[i] - 1)) for i in range(3)]

    def device(*moves):
        there = list(place)
        for dim, upper in moves:
            there[dim] = there[dim] + (1 if upper else -1)
        return tuple(there)
    sides = [(able[dim][upper], device((dim, upper))) for dim in range(3) for upper in (1, 0)]
    corners = [(able[p][sp] & able[q][sq], device((p, sp), (q, sq))) for p, q, sp, sq in EDGES]
    first = (4, 5, 2, 3, 0, 1)
    first_edges = (4, 5, 6, 7, 8, 9, 10, 11, 0, 1, 2, 3)

    barrier = pltpu.get_barrier_semaphore()
    for exists, there in sides + corners:
        @pl.when(exists)
        def _():
            pl.semaphore_signal(barrier, inc=1, device_id=there, device_id_type=pl.DeviceIdType.MESH)
    pl.semaphore_wait(barrier, sum(exists.astype(jnp.int32) for exists, there in sides + corners))
    for d, (exists, there) in enumerate(sides):
        @pl.when(jnp.logical_not(exists))
        def _():
            in_face[:, d] = jnp.zeros((SLOTS, 64, 128), f32)
            in_mat[:, d] = jnp.zeros((3, 32, 128), f32)
    for e, (exists, there) in enumerate(corners):
        @pl.when(jnp.logical_not(exists))
        def _():
            in_edge[:, e] = jnp.zeros((SLOTS, 8, 128), f32)

    def remote(src, dst, send, recv, there):
        return pltpu.make_async_remote_copy(
            src_ref=src, dst_ref=dst, send_sem=send, recv_sem=recv,
            device_id=there, device_id_type=pl.DeviceIdType.MESH)

    def face_copy(d, land, slot, rows, raw):
        rows = pl.ds(0, rows)
        return remote(
            out_face.at[slot, 0 if raw else d, rows], in_face.at[slot, land, rows],
            send_face.at[slot, d], recv_face.at[slot, land], sides[d][1])

    def edge_copy(e, land, slot, raw):
        src = out_face.at[slot, 0, pl.ds(0, 8)] if raw else out_edge.at[slot, e]
        return remote(src, in_edge.at[slot, land], send_edge.at[slot, e], recv_edge.at[slot, land], corners[e][1])

    def mat_copy(d, land, level):
        rows = pl.ds(0, FACE_ROWS[level])
        return remote(
            out_mat.at[level, d, rows], in_mat.at[level, land, rows],
            send_mat.at[level, d], recv_mat.at[level, land], sides[d][1])

    row = lax.broadcasted_iota(jnp.int32, (512, 512), 0)
    col = lax.broadcasted_iota(jnp.int32, (512, 512), 1)
    order[...] = jnp.where(element_of_row(row) == col, 1.0, 0.0).astype(bf16)
    m0[...] = lax.dot_general(
        order[...], jnp.broadcast_to(fine_ref[...].astype(f32), (128, 512)).astype(bf16),
        (((1,), (1,)), ((), ())), preferred_element_type=f32)
    m1[...] = spread_materials(mid_ref[...], 64, middle_of_row)
    m2[...] = spread_materials(coarse_ref[...], 8, lambda r: r)
    for level, m in enumerate((m0, m1, m2)):
        tiles = own_tiles(m[...] + 1.0, level)
        for d in first:
            packed = tiles if level == 2 else pack_face(tiles, level, d // 2, 1 - d % 2, 1)
            out_mat[level, d, :FACE_ROWS[level]] = packed
    for level in range(3):
        for d in first:
            @pl.when(sides[d][0])
            def _():
                mat_copy(d, d ^ 1, level).start()

    prepare(diag_ref, face_ref, prolong_ref, sweep_w, rest_w, inv_w, restrict_w, prolong_w)
    source = jnp.concatenate([rhs_ref[...], rhs_ref[...]], axis=0)
    total = None
    for piece in three(source):
        part = lax.dot_general(order[...], piece, (((1,), (1,)), ((), ())), preferred_element_type=f32)
        total = part if total is None else total + part
    f0[...] = total

    def scaled_inverse(value, material):
        return chosen(twice(split(value).astype(bf16), inv_w), material)

    g0[...] = scaled_inverse(f0[...], m0[...])
    v0[...] = g0[...]
    state = ((v0, g0, m0), (v1, g1, m1), (v2, g2, m2))
    halos = ((halo_g0, halo_m0), (halo_g1, halo_m1), (halo_g2, halo_m2))

    def merged(read, level, dim, layer):
        above = unpack_face(read(2 * dim), level, dim, 1, layer)
        below = unpack_face(read(2 * dim + 1), level, dim, 0, layer)
        return jnp.where(bit_is(dim, 1), above, below)

    def exchange(level, step, deep):
        slot = lax.rem(step, SLOTS)
        rows = FACE_ROWS[level]
        raw = level == 2
        layers = 2 if deep and not raw else 1
        value = state[level][0][...]
        tiles = own_tiles(value, level)
        if raw:
            out_face[slot, 0, :8] = value
        else:
            for d in first:
                for layer in range(layers):
                    out_face[slot, d, layer * rows:layer * rows + rows] = pack_face(
                        tiles, level, d // 2, 1 - d % 2, layer + 1)
                @pl.when(sides[d][0])
                def _():
                    face_copy(d, d ^ 1, slot, layers * rows, raw).start()
            if deep:
                for e in first_edges:
                    out_edge[slot, e] = pack_edge(tiles, level, *EDGES[e])
        if raw:
            for d in first:
                @pl.when(sides[d][0])
                def _():
                    face_copy(d, d ^ 1, slot, layers * rows, raw).start()
        if deep:
            for e in first_edges:
                @pl.when(corners[e][0])
                def _():
                    edge_copy(e, e ^ 3, slot, raw).start()
        u = split(value)
        if level == 0:
            for d in range(6):
                place_inner(lhs, u, d)
            lhs[6] = u.reshape(2, 2, 2, 2, 2, 16, 128).astype(bf16)
        for d in range(6):
            @pl.when(sides[d][0])
            def _():
                face_copy(d, d, slot, layers * rows, raw).wait_recv()
        if deep:
            for e in range(12):
                @pl.when(corners[e][0])
                def _():
                    edge_copy(e, e, slot, raw).wait_recv()
        near = [merged(lambda d: in_face[slot, d, :rows], level, dim, 1) for dim in range(3)]
        far, edges = None, None
        if deep:
            at = 0 if raw else rows
            far = [
                split_tiles(merged(lambda d: in_face[slot, d, at:at + rows], level, dim, 2)) for dim in range(3)
            ]
            edges = []
            for p, q in PAIRS:
                got = [
                    unpack_edge(in_edge[slot, e], level, p, q, sp, sq)
                    for e, (p_, q_, sp, sq) in enumerate(EDGES) if (p_, q_) == (p, q)
                ]
                got = [jnp.where(bit_is(q, 1), got[1], got[0]), jnp.where(bit_is(q, 1), got[3], got[2])]
                edges.append(split_tiles(jnp.where(bit_is(p, 1), got[1], got[0])))
        for d in range(6):
            @pl.when(sides[d][0])
            def _():
                face_copy(d, d ^ 1, slot, layers * rows, raw).wait_send()
        if deep:
            for e in range(12):
                @pl.when(corners[e][0])
                def _():
                    edge_copy(e, e ^ 3, slot, raw).wait_send()
        return u, near, far, edges

    def gathered(level, u, planes):
        if level == 0:
            for d in range(6):
                place_border(lhs, u, d, planes[d // 2])
            return [lhs[d].reshape(512, 128) for d in range(7)]
        fields = []
        for d in range(6):
            dim = d // 2
            field = shifted(own_tiles(u, level), (dim,) if level == 1 else (), dim, d % 2 == 0, planes[dim])
            fields.append(field.reshape(-1, 128))
        fields.append(u)
        if level == 2:
            fields = [jnp.concatenate([field, field], axis=0) for field in fields]
        return [field.astype(bf16) for field in fields]

    def relaxed(level, value, u, planes):
        v, g, m = state[level]
        product = twice(jnp.concatenate(gathered(level, u, planes)[:6], axis=1), sweep_w)
        return (1.0 - WEIGHT) * value + g[...] + chosen(product[:ROWS[level]], m[...])

    def residual(level, u, planes):
        f = (f0, f1)[level]
        product = twice(jnp.concatenate(gathered(level, u, planes), axis=1), rest_w)
        return f[...] - chosen(product, state[level][2][...])

    def refilled(u):
        for d in range(6):
            place_inner(lhs, u, d)
        lhs[6] = u.reshape(2, 2, 2, 2, 2, 16, 128).astype(bf16)

    def double_step(level, step, fresh, last):
        v = state[level][0]
        halo_g, halo_m = halos[level]
        u, near, far, edges = exchange(level, step, True)
        planes = [split_tiles(tiles) for tiles in near]
        raw = jnp.concatenate([tiles.reshape(-1, 128) for tiles in near], axis=0)
        if fresh:
            halo_g[...] = raw
        rows = [halo_fields(u, level, dim, planes[dim], far[dim], edges) for dim in range(3)]
        rows = jnp.concatenate(rows, axis=0)
        count = rows.shape[0]
        if count % 16:
            rows = jnp.concatenate([rows, rows[:16 - count % 16]], axis=0)
        value = relaxed(level, v[...], u, planes)
        product = twice(rows.astype(bf16), sweep_w)[:count]
        raw = (1.0 - WEIGHT) * raw + halo_g[...] + chosen(product, halo_m[...])
        planes = split(raw).reshape(3, -1, 8, 128)
        planes = [planes[dim] for dim in range(3)]
        u = split(value)
        if level == 0:
            refilled(u)
        if last == "sweep":
            v[...] = relaxed(level, value, u, planes)
            return None
        v[...] = value
        return residual(level, u, planes)

    def single_step(level, step, last):
        v = state[level][0]
        u, near, far, edges = exchange(level, step, False)
        planes = [split_tiles(tiles) for tiles in near]
        if last == "sweep":
            v[...] = relaxed(level, v[...], u, planes)
            return None
        return residual(level, u, planes)

    def coarser(value):
        u = split(value)
        count = u.shape[0] // 8
        parts = [u[c * count:(c + 1) * count] for c in range(8)]
        if count == 8:
            parts = [jnp.concatenate([part, part], axis=0) for part in parts]
        return twice(jnp.concatenate(parts, axis=1).astype(bf16), restrict_w)[:count]

    def finer(value):
        u = split(value)
        count = u.shape[0]
        if count == 8:
            u = jnp.concatenate([u, u], axis=0)
        product = twice(u.astype(bf16), prolong_w)[:count]
        return jnp.concatenate([product[:, c * 128:(c + 1) * 128] for c in range(8)], axis=0)

    def wide(value):
        return jnp.concatenate([value, value], axis=0)

    for level in range(3):
        for d in range(6):
            @pl.when(sides[d][0])
            def _():
                mat_copy(d, d, level).wait_recv()
                mat_copy(d, d ^ 1, level).wait_send()
        planes = [
            merged(lambda d: in_mat[level, d, :FACE_ROWS[level]], level, dim, 1).reshape(-1, 128)
            for dim in range(3)
        ]
        halos[level][1][...] = jnp.concatenate(planes, axis=0) - 1.0

    @pl.loop(0, CYCLES)
    def _(cycle):
        @pl.when(cycle == 0)
        def _():
            f1[...] = coarser(double_step(0, 0, True, "residual"))

        @pl.when(cycle > 0)
        def _():
            double_step(0, 6, False, "sweep")
            f1[...] = coarser(single_step(0, 7, "residual"))
        base = 1 + 7 * cycle
        g1[...] = scaled_inverse(f1[...], m1[...])
        v1[...] = g1[...]
        f2 = coarser(double_step(1, base, True, "residual"))
        g2[...] = scaled_inverse(wide(f2), wide(m2[...]))[:8]
        v2[...] = g2[...]
        double_step(2, base + 1, True, "sweep")
        single_step(2, base + 2, "sweep")
        v1[...] = v1[...] + finer(v2[...])
        double_step(1, base + 3, False, "sweep")
        v0[...] = v0[...] + finer(v1[...])
        double_step(0, base + 4, False, "sweep")

    result = jnp.transpose(v0[...])[:MODES]
    total = None
    for piece in three(result):
        part = jnp.dot(piece, order[...], preferred_element_type=f32)
        total = part if total is None else total + part
    out_ref[...] = total


def per_device(sizes, right_side, diag_blocks, face_blocks, prolong, mats_fine, mats_mid, mats_coarse):
    def vmem(shape, dtype=f32):
        return pltpu.VMEM(shape, dtype)
    field = [vmem((512, 128))] * 4
    middle = [vmem((64, 128))] * 4
    coarse = [vmem((8, 128))] * 3
    result = pl.pallas_call(
        partial(kernel, sizes),
        out_shape=jax.ShapeDtypeStruct((MODES, 512), f32),
        in_specs=[pl.BlockSpec(memory_space=pltpu.VMEM)] * 7,
        out_specs=pl.BlockSpec(memory_space=pltpu.VMEM),
        scratch_shapes=[
            vmem((2 * 768, 256), bf16),
            vmem((2 * 896, 256), bf16),
            vmem((2 * 128, 256), bf16),
            vmem((2 * 1024, 128), bf16),
            vmem((2 * 128, 1024), bf16),
            vmem((512, 512), bf16),
            vmem((7, 2, 2, 2, 2, 2, 16, 128), bf16),
        ] + field + middle + coarse + [vmem((3 * n, 128)) for n in (128, 32, 8)] * 2 + [
            vmem((SLOTS, 6, 64, 128)),
            vmem((SLOTS, 6, 64, 128)),
            vmem((SLOTS, 12, 8, 128)),
            vmem((SLOTS, 12, 8, 128)),
            vmem((3, 6, 32, 128)),
            vmem((3, 6, 32, 128)),
        ] + [pltpu.SemaphoreType.DMA((SLOTS, n)) for n in (6, 6, 12, 12)] + [
            pltpu.SemaphoreType.DMA((3, 6)),
            pltpu.SemaphoreType.DMA((3, 6)),
        ],
        compiler_params=pltpu.CompilerParams(collective_id=0, has_side_effects=True),
        name="cycles",
    )(
        right_side[0, 0, 0], diag_blocks, face_blocks, prolong,
        mats_fine.reshape(1, -1), mats_mid.reshape(1, -1), mats_coarse.reshape(1, -1),
    )
    return result[None, None, None]


def solution(mesh):
    placed = (
        P("gx", "gy", "gz", None, None),
        P(),
        P(),
        P(),
        P("gx", "gy", "gz", None),
        P("gx", "gy", "gz", None),
        P("gx", "gy", "gz", None),
    )
    sizes = tuple(mesh.shape[axis] for axis in AXES)
    return jax.shard_map(
        partial(per_device, sizes),
        mesh=mesh,
        in_specs=placed,
        out_specs=P("gx", "gy", "gz", None, None),
        check_vma=False,
    )
```

```python
from functools import partial

import jax
import jax.numpy as jnp
from jax import lax
from jax.experimental import pallas as pl
from jax.experimental.pallas import tpu as pltpu
from jax.sharding import PartitionSpec as P

MODES = 64
MATERIALS = 4
SWEEPS = 2
COARSE_SWEEPS = 4
CYCLES = 2
ROWS = (512, 64, 8)
TILE_DIMS = ((2, 2, 2, 2, 2, 2), (2, 2, 2), ())
FACE_ROWS = (32, 8, 8)
AXES = ("gx", "gy", "gz")
WEIGHT = 0.7
SCALE = 0.6
SUB = (4, 2, 1)
f32 = jnp.float32
bf16 = jnp.bfloat16
highest = lax.Precision.HIGHEST


def lanes(rows):
    return lax.broadcasted_iota(jnp.int32, (rows, 128), 1)


def swap_halves(x):
    return pltpu.roll(x, 64, axis=1)


def split(x):
    high = x.astype(bf16).astype(f32)
    return jnp.where(lanes(x.shape[0]) < 64, high, x - high)


def bit_is(dim, value):
    sub = lax.broadcasted_iota(jnp.int32, (8, 128), 0)
    return (jnp.right_shift(sub, 2 - dim) & 1) == value


def roll_sub(x, amount):
    shape = x.shape
    return pltpu.roll(x.reshape(-1, 8, 128), (-amount) % 8, axis=1).reshape(shape)


def pair(weights):
    high = weights.astype(bf16)
    return high, (weights - high.astype(f32)).astype(bf16)


def chosen(product, material):
    rows = product.shape[0]
    half = jnp.where(lanes(rows) < 64, 0.0, 1.0)
    offset = material - half
    kept = jnp.where(offset == 0.0, product[:, :128], jnp.where(offset == 2.0, product[:, 128:], 0.0))
    return kept + swap_halves(kept)


def twice(x, w_ref):
    return jnp.dot(jnp.concatenate([x, x], axis=1), w_ref[...], preferred_element_type=f32)


def three(x):
    a = x.astype(bf16)
    rest = x - a.astype(f32)
    b = rest.astype(bf16)
    return a, b, (rest - b.astype(f32)).astype(bf16)


def element_of_row(row):
    def bit(n):
        return jnp.right_shift(row, n) & 1
    x = bit(8) + 2 * bit(5) + 4 * bit(2)
    y = bit(7) + 2 * bit(4) + 4 * bit(1)
    z = bit(6) + 2 * bit(3) + 4 * bit(0)
    return x * 64 + y * 8 + z


def middle_of_row(row):
    def bit(n):
        return jnp.right_shift(row, n) & 1
    x = bit(5) + 2 * bit(2)
    y = bit(4) + 2 * bit(1)
    z = bit(3) + 2 * bit(0)
    return x * 16 + y * 4 + z


def spread_materials(mats, rows, place):
    row = lax.broadcasted_iota(jnp.int32, (rows, rows), 0)
    col = lax.broadcasted_iota(jnp.int32, (rows, rows), 1)
    kept = jnp.where(place(row) == col, jnp.broadcast_to(mats.astype(f32), (rows, rows)), 0.0)
    return jnp.broadcast_to(jnp.sum(kept, axis=1, keepdims=True), (rows, 128))


def invert(blocks):
    row_id = lax.broadcasted_iota(jnp.int32, blocks.shape, 1)
    lane_id = lax.broadcasted_iota(jnp.int32, blocks.shape, 2)
    for k in range(MODES):
        pivot = 1.0 / blocks[:, k:k + 1, k:k + 1]
        at_lane = lane_id == k
        row = jnp.where(at_lane[:, :1, :], 1.0, blocks[:, k:k + 1, :]) * pivot
        column = blocks[:, :, k:k + 1]
        rest = jnp.where(at_lane, 0.0, blocks) - column * row
        blocks = jnp.where(row_id == k, row, rest)
    return blocks


def prepare(diag_ref, face_ref, prolong_ref, sweep_w, rest_w, inv_w, restrict_w, prolong_w):
    inverse = invert(diag_ref[...])

    def side(parts):
        return jnp.concatenate(parts, axis=1)

    def store(ref, at, w):
        high, low = pair(w)
        half = ref.shape[0] // 2
        ref[at:at + 128] = jnp.concatenate([high, high], axis=0)
        ref[half + at:half + at + 128] = jnp.concatenate([low, low], axis=0)
    store(inv_w, 0, WEIGHT * side([inverse[m] for m in range(MATERIALS)]))
    store(rest_w, 6 * 128, side([diag_ref[m] for m in range(MATERIALS)]))
    for d in range(6):
        turned = [jnp.transpose(face_ref[d, m]) for m in range(MATERIALS)]
        store(rest_w, d * 128, side(turned))
        mixed = [
            jnp.dot(turned[m], inverse[m], precision=highest, preferred_element_type=f32)
            for m in range(MATERIALS)
        ]
        store(sweep_w, d * 128, -WEIGHT * side(mixed))
    for c in range(8):
        block = SCALE * prolong_ref[c]
        store(restrict_w, c * 128, side([block, block]))
        back = jnp.transpose(prolong_ref[c])
        high, low = pair(side([back, back]))
        columns = slice(c * 128, c * 128 + 128)
        prolong_w[0:128, columns] = jnp.concatenate([high, high], axis=0)
        prolong_w[128:256, columns] = jnp.concatenate([low, low], axis=0)


def index_at(level, dim, *bits):
    at = [slice(None)] * len(TILE_DIMS[level])
    for i, b in enumerate(bits):
        at[3 * i + dim] = b
    return tuple(at)


def depth(level):
    return 2 - level


PAIRS = ((0, 1), (0, 2), (1, 2))
EDGES = tuple((p, q, sp, sq) for p, q in PAIRS for sp in (0, 1) for sq in (0, 1))
SLOTS = 3


def own_tiles(value, level):
    return value.reshape(TILE_DIMS[level] + (8, 128))


def outer(tiles, level, dim, upper, layer):
    bits = [upper] * depth(level)
    if layer == 2 and bits:
        bits[0] = 1 - upper
    return tiles[index_at(level, dim, *bits)].reshape(-1, 8, 128)


def toward(dim, upper):
    return SUB[dim] if upper else -SUB[dim]


def two_halves(packed):
    other = swap_halves(packed.reshape(-1, 128)).reshape(packed.shape)
    low_lanes = lanes(8) < 64
    return jnp.concatenate([jnp.where(low_lanes, packed, other), jnp.where(low_lanes, other, packed)], axis=0)


def pack_face(tiles, level, dim, upper, layer):
    tiles = outer(tiles, level, dim, upper, layer)
    half = tiles.shape[0] // 2
    packed = jnp.where(bit_is(dim, 1 - upper), roll_sub(tiles[:half], toward(dim, upper)), tiles[half:])
    half = half // 2
    return jnp.where(lanes(8) < 64, packed[:half], packed[half:]).reshape(-1, 128)


def unpack_face(packed, level, dim, upper, layer):
    packed = packed.reshape(-1, 8, 128)
    if level == 2:
        return packed if layer == 2 else roll_sub(packed, -toward(dim, upper))
    both = two_halves(packed)
    return jnp.concatenate([both, roll_sub(both, -toward(dim, upper))], axis=0)


def pack_edge(tiles, level, p, q, sp, sq):
    at = list(index_at(level, p, *([sp] * depth(level))))
    for i, b in enumerate(index_at(level, q, *([sq] * depth(level)))):
        at[i] = b if at[i] == slice(None) else at[i]
    tiles = tiles[tuple(at)].reshape(-1, 8, 128)
    half = tiles.shape[0] // 2
    if level == 0:
        moved = roll_sub(tiles[:half], toward(p, sp) + toward(q, sq))
        tiles = jnp.where(bit_is(p, 1 - sp), moved, roll_sub(tiles[half:], toward(q, sq)))
    else:
        tiles = roll_sub(tiles, toward(p, sp) + toward(q, sq))
    return jnp.where(lanes(8) < 64, tiles[0], tiles[1])


def unpack_edge(packed, level, p, q, sp, sq):
    packed = packed.reshape(1, 8, 128)
    if level == 2:
        return roll_sub(packed, -toward(p, sp) - toward(q, sq))
    both = two_halves(packed)
    if level == 1:
        return both
    return jnp.concatenate([both, roll_sub(both, -toward(p, sp))], axis=0)


def split_tiles(tiles):
    return split(tiles.reshape(-1, 128)).reshape(tiles.shape)


def border(tiles, halo, dim, up):
    rolled = roll_sub(tiles, SUB[dim] if up else -SUB[dim])
    return jnp.where(bit_is(dim, 0 if up else 1), rolled, halo.reshape(tiles.shape))


def take(tiles, axis, bit):
    at = [slice(None)] * tiles.ndim
    at[axis] = bit
    return tiles[tuple(at)]


def shifted(tiles, axes, dim, up, halo):
    if not axes:
        return border(tiles, halo, dim, up)
    near, far = (0, 1) if up else (1, 0)

    def ordered(at_near, at_far, axis):
        return jnp.stack([at_near, at_far] if up else [at_far, at_near], axis=axis)
    if len(axes) == 1:
        return ordered(take(tiles, axes[0], far), border(take(tiles, axes[0], near), halo, dim, up), axes[0])
    kept = take(tiles, axes[0], near)
    deeper = axes[1] - 1
    end = border(take(kept, deeper, near), halo, dim, up)
    return ordered(take(tiles, axes[0], far), ordered(take(kept, deeper, far), end, deeper), axes[0])


def place_inner(lhs, u, d):
    dim, up = d // 2, d % 2 == 0
    tiles = own_tiles(u, 0)
    near, far = (0, 1) if up else (1, 0)

    def put(where, value):
        shape = value.shape[:-3] + (16, 128)
        lhs[(d,) + where] = value.reshape(shape).astype(bf16)
    put(index_at(0, dim, near)[:5], tiles[index_at(0, dim, far)])
    if dim < 2:
        put(index_at(0, dim, far, near)[:5], tiles[index_at(0, dim, near, far)])


def place_border(lhs, u, d, halo):
    dim, up = d // 2, d % 2 == 0
    tiles = own_tiles(u, 0)
    near, far = (0, 1) if up else (1, 0)
    edge = border(tiles[index_at(0, dim, near, near)], halo, dim, up)
    if dim < 2:
        lhs[(d,) + index_at(0, dim, far, far)[:5]] = edge.reshape(edge.shape[:-3] + (16, 128)).astype(bf16)
    else:
        inner = tiles[index_at(0, dim, near, far)]
        both = [inner, edge] if up else [edge, inner]
        both = jnp.concatenate(both, axis=-2)
        lhs[d, :, :, far] = both.astype(bf16)


def halo_fields(u, level, dim, near, far, edges):
    tiles = own_tiles(u, level)
    others = [i for i in range(3) if i != dim]
    bits = near.reshape((2,) * (2 * depth(level)) + (8, 128))
    fields = []
    for d in range(6):
        along, up = d // 2, d % 2 == 0
        if along == dim:
            own = outer(tiles, level, dim, 0 if up else 1, 1)
            field = jnp.where(bit_is(dim, 1 if up else 0), far, own)
        else:
            axes = [others.index(along) + 2 * i for i in range(depth(level))]
            field = shifted(bits, axes, along, up, edges[PAIRS.index((min(dim, along), max(dim, along)))])
        fields.append(field.reshape(-1, 128))
    return jnp.concatenate(fields, axis=1)


def kernel(
    sizes, rhs_ref, diag_ref, face_ref, prolong_ref, fine_ref, mid_ref, coarse_ref, out_ref,
    sweep_w, rest_w, inv_w, restrict_w, prolong_w, order, lhs,
    v0, f0, g0, m0, v1, f1, g1, m1, v2, g2, m2,
    halo_g0, halo_g1, halo_g2, halo_m0, halo_m1, halo_m2,
    out_face, in_face, out_edge, in_edge, out_mat, in_mat,
    send_face, recv_face, send_edge, recv_edge, send_mat, recv_mat,
    rhs_box, fine_box, mid_box, coarse_box, result, send_block, recv_block,
):
    home = tuple(lax.axis_index(axis) for axis in AXES)
    run = sizes[1] // sizes[2]
    shift = run // 2

    def holder(x, y, z):
        along = lax.rem(y + shift + sizes[1], sizes[1])
        return x, z * run + lax.rem(along, run), along // run
    worker = holder(*home)
    along = home[2] * run + lax.rem(home[1], run)
    place = [home[0], lax.rem(along - shift + sizes[1], sizes[1]), home[1] // run]
    owner = tuple(place)
    able = [((place[i] > 0), (place[i] < sizes[i] - 1)) for i in range(3)]

    def device(*moves):
        there = list(place)
        for dim, upper in moves:
            there[dim] = there[dim] + (1 if upper else -1)
        return holder(*there)
    sides = [(able[dim][upper], device((dim, upper))) for dim in range(3) for upper in (1, 0)]
    corners = [(able[p][sp] & able[q][sq], device((p, sp), (q, sq))) for p, q, sp, sq in EDGES]
    first = (2, 3, 4, 5, 0, 1)
    first_edges = (8, 9, 10, 11, 0, 1, 2, 3, 4, 5, 6, 7)

    barrier = pltpu.get_barrier_semaphore()
    for exists, there in sides + corners:
        @pl.when(exists)
        def _():
            pl.semaphore_signal(barrier, inc=1, device_id=there, device_id_type=pl.DeviceIdType.MESH)
    for there in (worker, owner):
        pl.semaphore_signal(barrier, inc=1, device_id=there, device_id_type=pl.DeviceIdType.MESH)
    pl.semaphore_wait(barrier, 2 + sum(exists.astype(jnp.int32) for exists, there in sides + corners))

    def remote(src, dst, send, recv, there):
        return pltpu.make_async_remote_copy(
            src_ref=src, dst_ref=dst, send_sem=send, recv_sem=recv,
            device_id=there, device_id_type=pl.DeviceIdType.MESH)
    moved = [
        remote(src, dst, send_block.at[i], recv_block.at[i], worker)
        for i, (src, dst) in enumerate((
            (fine_ref, fine_box), (mid_ref, mid_box), (coarse_ref, coarse_box), (rhs_ref, rhs_box)))
    ]
    for copy in moved:
        copy.start()
    for d, (exists, there) in enumerate(sides):
        @pl.when(jnp.logical_not(exists))
        def _():
            in_face[:, d] = jnp.zeros((SLOTS, 64, 128), f32)
            in_mat[:, d] = jnp.zeros((3, 32, 128), f32)
    for e, (exists, there) in enumerate(corners):
        @pl.when(jnp.logical_not(exists))
        def _():
            in_edge[:, e] = jnp.zeros((SLOTS, 8, 128), f32)

    def face_copy(d, land, slot, rows, raw):
        rows = pl.ds(0, rows)
        return remote(
            out_face.at[slot, 0 if raw else d, rows], in_face.at[slot, land, rows],
            send_face.at[slot, d], recv_face.at[slot, land], sides[d][1])

    def edge_copy(e, land, slot, raw):
        src = out_face.at[slot, 0, pl.ds(0, 8)] if raw else out_edge.at[slot, e]
        return remote(src, in_edge.at[slot, land], send_edge.at[slot, e], recv_edge.at[slot, land], corners[e][1])

    def mat_copy(d, land, level):
        rows = pl.ds(0, FACE_ROWS[level])
        return remote(
            out_mat.at[level, d, rows], in_mat.at[level, land, rows],
            send_mat.at[level, d], recv_mat.at[level, land], sides[d][1])

    row = lax.broadcasted_iota(jnp.int32, (512, 512), 0)
    col = lax.broadcasted_iota(jnp.int32, (512, 512), 1)
    order[...] = jnp.where(element_of_row(row) == col, 1.0, 0.0).astype(bf16)
    prepare(diag_ref, face_ref, prolong_ref, sweep_w, rest_w, inv_w, restrict_w, prolong_w)
    for copy in moved[:3]:
        copy.wait()
    m0[...] = lax.dot_general(
        order[...], jnp.broadcast_to(fine_box[...].astype(f32), (128, 512)).astype(bf16),
        (((1,), (1,)), ((), ())), preferred_element_type=f32)
    m1[...] = spread_materials(mid_box[...], 64, middle_of_row)
    m2[...] = spread_materials(coarse_box[...], 8, lambda r: r)
    for level, m in enumerate((m0, m1, m2)):
        tiles = own_tiles(m[...] + 1.0, level)
        for d in first:
            packed = tiles if level == 2 else pack_face(tiles, level, d // 2, 1 - d % 2, 1)
            out_mat[level, d, :FACE_ROWS[level]] = packed
    for level in range(3):
        for d in first:
            @pl.when(sides[d][0])
            def _():
                mat_copy(d, d ^ 1, level).start()

    moved[3].wait()
    source = jnp.concatenate([rhs_box[...], rhs_box[...]], axis=0)
    total = None
    for piece in three(source):
        part = lax.dot_general(order[...], piece, (((1,), (1,)), ((), ())), preferred_element_type=f32)
        total = part if total is None else total + part
    f0[...] = total

    def scaled_inverse(value, material):
        return chosen(twice(split(value).astype(bf16), inv_w), material)

    g0[...] = scaled_inverse(f0[...], m0[...])
    v0[...] = g0[...]
    state = ((v0, g0, m0), (v1, g1, m1), (v2, g2, m2))
    halos = ((halo_g0, halo_m0), (halo_g1, halo_m1), (halo_g2, halo_m2))

    def merged(read, level, dim, layer):
        above = unpack_face(read(2 * dim), level, dim, 1, layer)
        below = unpack_face(read(2 * dim + 1), level, dim, 0, layer)
        return jnp.where(bit_is(dim, 1), above, below)

    def exchange(level, step, deep):
        slot = lax.rem(step, SLOTS)
        rows = FACE_ROWS[level]
        raw = level == 2
        layers = 2 if deep and not raw else 1
        value = state[level][0][...]
        tiles = own_tiles(value, level)
        if raw:
            out_face[slot, 0, :8] = value
        if deep:
            for e in first_edges:
                if not raw:
                    out_edge[slot, e] = pack_edge(tiles, level, *EDGES[e])
                @pl.when(corners[e][0])
                def _():
                    edge_copy(e, e ^ 3, slot, raw).start()
        for d in first:
            for layer in range(0 if raw else layers):
                out_face[slot, d, layer * rows:layer * rows + rows] = pack_face(
                    tiles, level, d // 2, 1 - d % 2, layer + 1)
            @pl.when(sides[d][0])
            def _():
                face_copy(d, d ^ 1, slot, layers * rows, raw).start()
        u = split(value)
        if level == 0:
            for d in range(6):
                place_inner(lhs, u, d)
            lhs[6] = u.reshape(2, 2, 2, 2, 2, 16, 128).astype(bf16)
        for d in range(6):
            @pl.when(sides[d][0])
            def _():
                face_copy(d, d, slot, layers * rows, raw).wait_recv()
        if deep:
            for e in range(12):
                @pl.when(corners[e][0])
                def _():
                    edge_copy(e, e, slot, raw).wait_recv()
        near = [merged(lambda d: in_face[slot, d, :rows], level, dim, 1) for dim in range(3)]
        far, edges = None, None
        if deep:
            at = 0 if raw else rows
            far = [
                split_tiles(merged(lambda d: in_face[slot, d, at:at + rows], level, dim, 2)) for dim in range(3)
            ]
            edges = []
            for p, q in PAIRS:
                got = [
                    unpack_edge(in_edge[slot, e], level, p, q, sp, sq)
                    for e, (p_, q_, sp, sq) in enumerate(EDGES) if (p_, q_) == (p, q)
                ]
                got = [jnp.where(bit_is(q, 1), got[1], got[0]), jnp.where(bit_is(q, 1), got[3], got[2])]
                edges.append(split_tiles(jnp.where(bit_is(p, 1), got[1], got[0])))
        for d in range(6):
            @pl.when(sides[d][0])
            def _():
                face_copy(d, d ^ 1, slot, layers * rows, raw).wait_send()
        if deep:
            for e in range(12):
                @pl.when(corners[e][0])
                def _():
                    edge_copy(e, e ^ 3, slot, raw).wait_send()
        return u, near, far, edges

    def gathered(level, u, planes):
        if level == 0:
            for d in range(6):
                place_border(lhs, u, d, planes[d // 2])
            return [lhs[d].reshape(512, 128) for d in range(7)]
        fields = []
        for d in range(6):
            dim = d // 2
            field = shifted(own_tiles(u, level), (dim,) if level == 1 else (), dim, d % 2 == 0, planes[dim])
            fields.append(field.reshape(-1, 128))
        fields.append(u)
        if level == 2:
            fields = [jnp.concatenate([field, field], axis=0) for field in fields]
        return [field.astype(bf16) for field in fields]

    def relaxed(level, value, u, planes):
        v, g, m = state[level]
        product = twice(jnp.concatenate(gathered(level, u, planes)[:6], axis=1), sweep_w)
        return (1.0 - WEIGHT) * value + g[...] + chosen(product[:ROWS[level]], m[...])

    def residual(level, u, planes):
        f = (f0, f1)[level]
        product = twice(jnp.concatenate(gathered(level, u, planes), axis=1), rest_w)
        return f[...] - chosen(product, state[level][2][...])

    def refilled(u):
        for d in range(6):
            place_inner(lhs, u, d)
        lhs[6] = u.reshape(2, 2, 2, 2, 2, 16, 128).astype(bf16)

    def double_step(level, step, fresh, last):
        v = state[level][0]
        halo_g, halo_m = halos[level]
        u, near, far, edges = exchange(level, step, True)
        planes = [split_tiles(tiles) for tiles in near]
        raw = jnp.concatenate([tiles.reshape(-1, 128) for tiles in near], axis=0)
        if fresh:
            halo_g[...] = raw
        rows = [halo_fields(u, level, dim, planes[dim], far[dim], edges) for dim in range(3)]
        rows = jnp.concatenate(rows, axis=0)
        count = rows.shape[0]
        if count % 16:
            rows = jnp.concatenate([rows, rows[:16 - count % 16]], axis=0)
        value = relaxed(level, v[...], u, planes)
        product = twice(rows.astype(bf16), sweep_w)[:count]
        raw = (1.0 - WEIGHT) * raw + halo_g[...] + chosen(product, halo_m[...])
        planes = split(raw).reshape(3, -1, 8, 128)
        planes = [planes[dim] for dim in range(3)]
        u = split(value)
        if level == 0:
            refilled(u)
        if last == "sweep":
            v[...] = relaxed(level, value, u, planes)
            return None
        v[...] = value
        return residual(level, u, planes)

    def single_step(level, step, last):
        v = state[level][0]
        u, near, far, edges = exchange(level, step, False)
        planes = [split_tiles(tiles) for tiles in near]
        if last == "sweep":
            v[...] = relaxed(level, v[...], u, planes)
            return None
        return residual(level, u, planes)

    def coarser(value):
        u = split(value)
        count = u.shape[0] // 8
        parts = [u[c * count:(c + 1) * count] for c in range(8)]
        if count == 8:
            parts = [jnp.concatenate([part, part], axis=0) for part in parts]
        return twice(jnp.concatenate(parts, axis=1).astype(bf16), restrict_w)[:count]

    def finer(value):
        u = split(value)
        count = u.shape[0]
        if count == 8:
            u = jnp.concatenate([u, u], axis=0)
        product = twice(u.astype(bf16), prolong_w)[:count]
        return jnp.concatenate([product[:, c * 128:(c + 1) * 128] for c in range(8)], axis=0)

    def wide(value):
        return jnp.concatenate([value, value], axis=0)

    for level in range(3):
        for d in range(6):
            @pl.when(sides[d][0])
            def _():
                mat_copy(d, d, level).wait_recv()
                mat_copy(d, d ^ 1, level).wait_send()
        planes = [
            merged(lambda d: in_mat[level, d, :FACE_ROWS[level]], level, dim, 1).reshape(-1, 128)
            for dim in range(3)
        ]
        halos[level][1][...] = jnp.concatenate(planes, axis=0) - 1.0

    @pl.loop(0, CYCLES)
    def _(cycle):
        @pl.when(cycle == 0)
        def _():
            f1[...] = coarser(double_step(0, 0, True, "residual"))

        @pl.when(cycle > 0)
        def _():
            double_step(0, 6, False, "sweep")
            f1[...] = coarser(single_step(0, 7, "residual"))
        base = 1 + 7 * cycle
        g1[...] = scaled_inverse(f1[...], m1[...])
        v1[...] = g1[...]
        f2 = coarser(double_step(1, base, True, "residual"))
        g2[...] = scaled_inverse(wide(f2), wide(m2[...]))[:8]
        v2[...] = g2[...]
        double_step(2, base + 1, True, "sweep")
        single_step(2, base + 2, "sweep")
        v1[...] = v1[...] + finer(v2[...])
        double_step(1, base + 3, False, "sweep")
        v0[...] = v0[...] + finer(v1[...])
        double_step(0, base + 4, False, "sweep")

    pieces = three(jnp.transpose(v0[...])[:MODES])
    back = []
    for half in range(2):
        columns = pl.ds(256 * half, 256)
        total = None
        for piece in pieces:
            part = jnp.dot(piece, order[:, columns], preferred_element_type=f32)
            total = part if total is None else total + part
        result[half] = total
        back.append(remote(
            result.at[half], out_ref.at[:, columns], send_block.at[4 + half], recv_block.at[4 + half], owner))
        back[half].start()
    for copy in back:
        copy.wait()


def per_device(sizes, right_side, diag_blocks, face_blocks, prolong, mats_fine, mats_mid, mats_coarse):
    def vmem(shape, dtype=f32):
        return pltpu.VMEM(shape, dtype)
    field = [vmem((512, 128))] * 4
    middle = [vmem((64, 128))] * 4
    coarse = [vmem((8, 128))] * 3
    result = pl.pallas_call(
        partial(kernel, sizes),
        out_shape=jax.ShapeDtypeStruct((MODES, 512), f32),
        in_specs=[pl.BlockSpec(memory_space=pltpu.VMEM)] * 7,
        out_specs=pl.BlockSpec(memory_space=pltpu.VMEM),
        scratch_shapes=[
            vmem((2 * 768, 256), bf16),
            vmem((2 * 896, 256), bf16),
            vmem((2 * 128, 256), bf16),
            vmem((2 * 1024, 128), bf16),
            vmem((2 * 128, 1024), bf16),
            vmem((512, 512), bf16),
            vmem((7, 2, 2, 2, 2, 2, 16, 128), bf16),
        ] + field + middle + coarse + [vmem((3 * n, 128)) for n in (128, 32, 8)] * 2 + [
            vmem((SLOTS, 6, 64, 128)),
            vmem((SLOTS, 6, 64, 128)),
            vmem((SLOTS, 12, 8, 128)),
            vmem((SLOTS, 12, 8, 128)),
            vmem((3, 6, 32, 128)),
            vmem((3, 6, 32, 128)),
        ] + [pltpu.SemaphoreType.DMA((SLOTS, n)) for n in (6, 6, 12, 12)] + [
            pltpu.SemaphoreType.DMA((3, 6)),
            pltpu.SemaphoreType.DMA((3, 6)),
            vmem((64, 512)),
            vmem((1, 512), jnp.int32),
            vmem((1, 64), jnp.int32),
            vmem((1, 8), jnp.int32),
            vmem((2, 64, 256)),
            pltpu.SemaphoreType.DMA((6,)),
            pltpu.SemaphoreType.DMA((6,)),
        ],
        compiler_params=pltpu.CompilerParams(collective_id=0, has_side_effects=True),
        name="cycles",
    )(
        right_side[0, 0, 0], diag_blocks, face_blocks, prolong,
        mats_fine.reshape(1, -1), mats_mid.reshape(1, -1), mats_coarse.reshape(1, -1),
    )
    return result[None, None, None]


def solution(mesh):
    placed = (
        P("gx", "gy", "gz", None, None),
        P(),
        P(),
        P(),
        P("gx", "gy", "gz", None),
        P("gx", "gy", "gz", None),
        P("gx", "gy", "gz", None),
    )
    sizes = tuple(mesh.shape[axis] for axis in AXES)
    return jax.shard_map(
        partial(per_device, sizes),
        mesh=mesh,
        in_specs=placed,
        out_specs=P("gx", "gy", "gz", None, None),
        check_vma=False,
    )
```

```python
from functools import partial

import jax
import jax.numpy as jnp
from jax import lax
from jax.experimental import pallas as pl
from jax.experimental.pallas import tpu as pltpu
from jax.sharding import PartitionSpec as P

MODES = 64
MATERIALS = 4
SWEEPS = 2
COARSE_SWEEPS = 4
CYCLES = 2
ROWS = (512, 64, 8)
TILE_DIMS = ((2, 2, 2, 2, 2, 2), (2, 2, 2), ())
FACE_ROWS = (32, 8, 8)
AXES = ("gx", "gy", "gz")
WEIGHT = 0.7
SCALE = 0.6
SUB = (4, 2, 1)
f32 = jnp.float32
bf16 = jnp.bfloat16
highest = lax.Precision.HIGHEST


def lanes(rows):
    return lax.broadcasted_iota(jnp.int32, (rows, 128), 1)


def swap_halves(x):
    return pltpu.roll(x, 64, axis=1)


def split(x):
    high = x.astype(bf16).astype(f32)
    return jnp.where(lanes(x.shape[0]) < 64, high, x - high)


def bit_is(dim, value):
    sub = lax.broadcasted_iota(jnp.int32, (8, 128), 0)
    return (jnp.right_shift(sub, 2 - dim) & 1) == value


def roll_sub(x, amount):
    shape = x.shape
    return pltpu.roll(x.reshape(-1, 8, 128), (-amount) % 8, axis=1).reshape(shape)


def pair(weights):
    high = weights.astype(bf16)
    return high, (weights - high.astype(f32)).astype(bf16)


def chosen(product, material):
    rows = product.shape[0]
    half = jnp.where(lanes(rows) < 64, 0.0, 1.0)
    offset = material - half
    kept = jnp.where(offset == 0.0, product[:, :128], jnp.where(offset == 2.0, product[:, 128:], 0.0))
    return kept + swap_halves(kept)


def twice(x, w_ref):
    return jnp.dot(jnp.concatenate([x, x], axis=1), w_ref[...], preferred_element_type=f32)


def three(x):
    a = x.astype(bf16)
    rest = x - a.astype(f32)
    b = rest.astype(bf16)
    return a, b, (rest - b.astype(f32)).astype(bf16)


def element_of_row(row):
    def bit(n):
        return jnp.right_shift(row, n) & 1
    x = bit(8) + 2 * bit(5) + 4 * bit(2)
    y = bit(7) + 2 * bit(4) + 4 * bit(1)
    z = bit(6) + 2 * bit(3) + 4 * bit(0)
    return x * 64 + y * 8 + z


def middle_of_row(row):
    def bit(n):
        return jnp.right_shift(row, n) & 1
    x = bit(5) + 2 * bit(2)
    y = bit(4) + 2 * bit(1)
    z = bit(3) + 2 * bit(0)
    return x * 16 + y * 4 + z


def spread_materials(mats, rows, place):
    row = lax.broadcasted_iota(jnp.int32, (rows, rows), 0)
    col = lax.broadcasted_iota(jnp.int32, (rows, rows), 1)
    kept = jnp.where(place(row) == col, jnp.broadcast_to(mats.astype(f32), (rows, rows)), 0.0)
    return jnp.broadcast_to(jnp.sum(kept, axis=1, keepdims=True), (rows, 128))


def invert(blocks):
    row_id = lax.broadcasted_iota(jnp.int32, blocks.shape, 1)
    lane_id = lax.broadcasted_iota(jnp.int32, blocks.shape, 2)
    for k in range(MODES):
        pivot = 1.0 / blocks[:, k:k + 1, k:k + 1]
        at_lane = lane_id == k
        row = jnp.where(at_lane[:, :1, :], 1.0, blocks[:, k:k + 1, :]) * pivot
        column = blocks[:, :, k:k + 1]
        rest = jnp.where(at_lane, 0.0, blocks) - column * row
        blocks = jnp.where(row_id == k, row, rest)
    return blocks


def prepare(diag_ref, face_ref, prolong_ref, sweep_w, rest_w, inv_w, restrict_w, prolong_w):
    inverse = invert(diag_ref[...])

    def side(parts):
        return jnp.concatenate(parts, axis=1)

    def store(ref, at, w):
        high, low = pair(w)
        half = ref.shape[0] // 2
        ref[at:at + 128] = jnp.concatenate([high, high], axis=0)
        ref[half + at:half + at + 128] = jnp.concatenate([low, low], axis=0)
    store(inv_w, 0, WEIGHT * side([inverse[m] for m in range(MATERIALS)]))
    store(rest_w, 6 * 128, side([diag_ref[m] for m in range(MATERIALS)]))
    for d in range(6):
        turned = [jnp.transpose(face_ref[d, m]) for m in range(MATERIALS)]
        store(rest_w, d * 128, side(turned))
        mixed = [
            jnp.dot(turned[m], inverse[m], precision=highest, preferred_element_type=f32)
            for m in range(MATERIALS)
        ]
        store(sweep_w, d * 128, -WEIGHT * side(mixed))
    for c in range(8):
        block = SCALE * prolong_ref[c]
        store(restrict_w, c * 128, side([block, block]))
        back = jnp.transpose(prolong_ref[c])
        high, low = pair(side([back, back]))
        columns = slice(c * 128, c * 128 + 128)
        prolong_w[0:128, columns] = jnp.concatenate([high, high], axis=0)
        prolong_w[128:256, columns] = jnp.concatenate([low, low], axis=0)


def index_at(level, dim, *bits):
    at = [slice(None)] * len(TILE_DIMS[level])
    for i, b in enumerate(bits):
        at[3 * i + dim] = b
    return tuple(at)


def depth(level):
    return 2 - level


PAIRS = ((0, 1), (0, 2), (1, 2))
EDGES = tuple((p, q, sp, sq) for p, q in PAIRS for sp in (0, 1) for sq in (0, 1))
SLOTS = 3


def own_tiles(value, level):
    return value.reshape(TILE_DIMS[level] + (8, 128))


def outer(tiles, level, dim, upper, layer):
    bits = [upper] * depth(level)
    if layer == 2 and bits:
        bits[0] = 1 - upper
    return tiles[index_at(level, dim, *bits)].reshape(-1, 8, 128)


def toward(dim, upper):
    return SUB[dim] if upper else -SUB[dim]


def two_halves(packed):
    other = swap_halves(packed.reshape(-1, 128)).reshape(packed.shape)
    low_lanes = lanes(8) < 64
    return jnp.concatenate([jnp.where(low_lanes, packed, other), jnp.where(low_lanes, other, packed)], axis=0)


def pack_face(tiles, level, dim, upper, layer):
    tiles = outer(tiles, level, dim, upper, layer)
    half = tiles.shape[0] // 2
    packed = jnp.where(bit_is(dim, 1 - upper), roll_sub(tiles[:half], toward(dim, upper)), tiles[half:])
    half = half // 2
    return jnp.where(lanes(8) < 64, packed[:half], packed[half:]).reshape(-1, 128)


def unpack_face(packed, level, dim, upper, layer):
    packed = packed.reshape(-1, 8, 128)
    if level == 2:
        return packed if layer == 2 else roll_sub(packed, -toward(dim, upper))
    both = two_halves(packed)
    return jnp.concatenate([both, roll_sub(both, -toward(dim, upper))], axis=0)


def pack_edge(tiles, level, p, q, sp, sq):
    at = list(index_at(level, p, *([sp] * depth(level))))
    for i, b in enumerate(index_at(level, q, *([sq] * depth(level)))):
        at[i] = b if at[i] == slice(None) else at[i]
    tiles = tiles[tuple(at)].reshape(-1, 8, 128)
    half = tiles.shape[0] // 2
    if level == 0:
        moved = roll_sub(tiles[:half], toward(p, sp) + toward(q, sq))
        tiles = jnp.where(bit_is(p, 1 - sp), moved, roll_sub(tiles[half:], toward(q, sq)))
    else:
        tiles = roll_sub(tiles, toward(p, sp) + toward(q, sq))
    return jnp.where(lanes(8) < 64, tiles[0], tiles[1])


def unpack_edge(packed, level, p, q, sp, sq):
    packed = packed.reshape(1, 8, 128)
    if level == 2:
        return roll_sub(packed, -toward(p, sp) - toward(q, sq))
    both = two_halves(packed)
    if level == 1:
        return both
    return jnp.concatenate([both, roll_sub(both, -toward(p, sp))], axis=0)


def split_tiles(tiles):
    return split(tiles.reshape(-1, 128)).reshape(tiles.shape)


def border(tiles, halo, dim, up):
    rolled = roll_sub(tiles, SUB[dim] if up else -SUB[dim])
    return jnp.where(bit_is(dim, 0 if up else 1), rolled, halo.reshape(tiles.shape))


def take(tiles, axis, bit):
    at = [slice(None)] * tiles.ndim
    at[axis] = bit
    return tiles[tuple(at)]


def shifted(tiles, axes, dim, up, halo):
    if not axes:
        return border(tiles, halo, dim, up)
    near, far = (0, 1) if up else (1, 0)

    def ordered(at_near, at_far, axis):
        return jnp.stack([at_near, at_far] if up else [at_far, at_near], axis=axis)
    if len(axes) == 1:
        return ordered(take(tiles, axes[0], far), border(take(tiles, axes[0], near), halo, dim, up), axes[0])
    kept = take(tiles, axes[0], near)
    deeper = axes[1] - 1
    end = border(take(kept, deeper, near), halo, dim, up)
    return ordered(take(tiles, axes[0], far), ordered(take(kept, deeper, far), end, deeper), axes[0])


def place_inner(lhs, u, d):
    dim, up = d // 2, d % 2 == 0
    tiles = own_tiles(u, 0)
    near, far = (0, 1) if up else (1, 0)

    def put(where, value):
        shape = value.shape[:-3] + (16, 128)
        lhs[(d,) + where] = value.reshape(shape).astype(bf16)
    put(index_at(0, dim, near)[:5], tiles[index_at(0, dim, far)])
    if dim < 2:
        put(index_at(0, dim, far, near)[:5], tiles[index_at(0, dim, near, far)])


def place_border(lhs, u, d, halo):
    dim, up = d // 2, d % 2 == 0
    tiles = own_tiles(u, 0)
    near, far = (0, 1) if up else (1, 0)
    edge = border(tiles[index_at(0, dim, near, near)], halo, dim, up)
    if dim < 2:
        lhs[(d,) + index_at(0, dim, far, far)[:5]] = edge.reshape(edge.shape[:-3] + (16, 128)).astype(bf16)
    else:
        inner = tiles[index_at(0, dim, near, far)]
        both = [inner, edge] if up else [edge, inner]
        both = jnp.concatenate(both, axis=-2)
        lhs[d, :, :, far] = both.astype(bf16)


def halo_fields(u, level, dim, near, far, edges):
    tiles = own_tiles(u, level)
    others = [i for i in range(3) if i != dim]
    bits = near.reshape((2,) * (2 * depth(level)) + (8, 128))
    fields = []
    for d in range(6):
        along, up = d // 2, d % 2 == 0
        if along == dim:
            own = outer(tiles, level, dim, 0 if up else 1, 1)
            field = jnp.where(bit_is(dim, 1 if up else 0), far, own)
        else:
            axes = [others.index(along) + 2 * i for i in range(depth(level))]
            field = shifted(bits, axes, along, up, edges[PAIRS.index((min(dim, along), max(dim, along)))])
        fields.append(field.reshape(-1, 128))
    return jnp.concatenate(fields, axis=1)


def kernel(
    sizes, rhs_ref, diag_ref, face_ref, prolong_ref, fine_ref, mid_ref, coarse_ref, out_ref,
    sweep_w, rest_w, inv_w, restrict_w, prolong_w, order, lhs,
    v0, f0, g0, m0, v1, f1, g1, m1, v2, g2, m2,
    halo_g0, halo_g1, halo_g2, halo_m0, halo_m1, halo_m2,
    out_face, in_face, out_edge, in_edge, out_mat, in_mat,
    send_face, recv_face, send_edge, recv_edge, send_mat, recv_mat,
    rhs_box, fine_box, mid_box, coarse_box, result, send_block, recv_block, inner,
):
    home = tuple(lax.axis_index(axis) for axis in AXES)
    run = sizes[1] // sizes[2]
    shift = run // 2

    def holder(x, y, z):
        along = lax.rem(y + shift + sizes[1], sizes[1])
        return x, z * run + lax.rem(along, run), along // run
    worker = holder(*home)
    along = home[2] * run + lax.rem(home[1], run)
    place = [home[0], lax.rem(along - shift + sizes[1], sizes[1]), home[1] // run]
    owner = tuple(place)
    able = [((place[i] > 0), (place[i] < sizes[i] - 1)) for i in range(3)]

    def device(*moves):
        there = list(place)
        for dim, upper in moves:
            there[dim] = there[dim] + (1 if upper else -1)
        return holder(*there)
    sides = [(able[dim][upper], device((dim, upper))) for dim in range(3) for upper in (1, 0)]
    corners = [(able[p][sp] & able[q][sq], device((p, sp), (q, sq))) for p, q, sp, sq in EDGES]
    first = (2, 3, 4, 5, 0, 1)
    first_edges = (8, 9, 10, 11, 0, 1, 2, 3, 4, 5, 6, 7)

    barrier = pltpu.get_barrier_semaphore()
    for exists, there in sides + corners:
        @pl.when(exists)
        def _():
            pl.semaphore_signal(barrier, inc=1, device_id=there, device_id_type=pl.DeviceIdType.MESH)
    for there in (worker, owner):
        pl.semaphore_signal(barrier, inc=1, device_id=there, device_id_type=pl.DeviceIdType.MESH)
    pl.semaphore_wait(barrier, 2 + sum(exists.astype(jnp.int32) for exists, there in sides + corners))

    def remote(src, dst, send, recv, there):
        return pltpu.make_async_remote_copy(
            src_ref=src, dst_ref=dst, send_sem=send, recv_sem=recv,
            device_id=there, device_id_type=pl.DeviceIdType.MESH)
    moved = [
        remote(src, dst, send_block.at[i], recv_block.at[i], worker)
        for i, (src, dst) in enumerate((
            (fine_ref, fine_box), (mid_ref, mid_box), (coarse_ref, coarse_box), (rhs_ref, rhs_box)))
    ]
    for copy in moved:
        copy.start()
    for d, (exists, there) in enumerate(sides):
        @pl.when(jnp.logical_not(exists))
        def _():
            in_face[:, d] = jnp.zeros((SLOTS, 64, 128), f32)
            in_mat[:, d] = jnp.zeros((3, 32, 128), f32)
    for e, (exists, there) in enumerate(corners):
        @pl.when(jnp.logical_not(exists))
        def _():
            in_edge[:, e] = jnp.zeros((SLOTS, 8, 128), f32)

    def face_copy(d, land, slot, rows, raw):
        rows = pl.ds(0, rows)
        return remote(
            out_face.at[slot, 0 if raw else d, rows], in_face.at[slot, land, rows],
            send_face.at[slot, d], recv_face.at[slot, land], sides[d][1])

    def edge_copy(e, land, slot, raw):
        src = out_face.at[slot, 0, pl.ds(0, 8)] if raw else out_edge.at[slot, e]
        return remote(src, in_edge.at[slot, land], send_edge.at[slot, e], recv_edge.at[slot, land], corners[e][1])

    def mat_copy(d, land, level):
        rows = pl.ds(0, FACE_ROWS[level])
        return remote(
            out_mat.at[level, d, rows], in_mat.at[level, land, rows],
            send_mat.at[level, d], recv_mat.at[level, land], sides[d][1])

    row = lax.broadcasted_iota(jnp.int32, (512, 512), 0)
    col = lax.broadcasted_iota(jnp.int32, (512, 512), 1)
    order[...] = jnp.where(element_of_row(row) == col, 1.0, 0.0).astype(bf16)
    prepare(diag_ref, face_ref, prolong_ref, sweep_w, rest_w, inv_w, restrict_w, prolong_w)
    for copy in moved[:3]:
        copy.wait()
    m0[...] = lax.dot_general(
        order[...], jnp.broadcast_to(fine_box[...].astype(f32), (128, 512)).astype(bf16),
        (((1,), (1,)), ((), ())), preferred_element_type=f32)
    m1[...] = spread_materials(mid_box[...], 64, middle_of_row)
    m2[...] = spread_materials(coarse_box[...], 8, lambda r: r)
    for level, m in enumerate((m0, m1, m2)):
        tiles = own_tiles(m[...] + 1.0, level)
        for d in first:
            packed = tiles if level == 2 else pack_face(tiles, level, d // 2, 1 - d % 2, 1)
            out_mat[level, d, :FACE_ROWS[level]] = packed
    for level in range(3):
        for d in first:
            @pl.when(sides[d][0])
            def _():
                mat_copy(d, d ^ 1, level).start()

    moved[3].wait()
    source = jnp.concatenate([rhs_box[...], rhs_box[...]], axis=0)
    total = None
    for piece in three(source):
        part = lax.dot_general(order[...], piece, (((1,), (1,)), ((), ())), preferred_element_type=f32)
        total = part if total is None else total + part
    f0[...] = total

    def scaled_inverse(value, material):
        return chosen(twice(split(value).astype(bf16), inv_w), material)

    g0[...] = scaled_inverse(f0[...], m0[...])
    v0[...] = g0[...]
    state = ((v0, g0, m0), (v1, g1, m1), (v2, g2, m2))
    halos = ((halo_g0, halo_m0), (halo_g1, halo_m1), (halo_g2, halo_m2))

    def merged(read, level, dim, layer):
        above = unpack_face(read(2 * dim), level, dim, 1, layer)
        below = unpack_face(read(2 * dim + 1), level, dim, 0, layer)
        return jnp.where(bit_is(dim, 1), above, below)

    def exchange(level, step, deep, weights):
        slot = lax.rem(step, SLOTS)
        rows = FACE_ROWS[level]
        raw = level == 2
        layers = 2 if deep and not raw else 1
        value = state[level][0][...]
        tiles = own_tiles(value, level)
        if raw:
            out_face[slot, 0, :8] = value
        if not raw:
            for e in first_edges if deep else ():
                out_edge[slot, e] = pack_edge(tiles, level, *EDGES[e])
            for d in first:
                for layer in range(layers):
                    out_face[slot, d, layer * rows:layer * rows + rows] = pack_face(
                        tiles, level, d // 2, 1 - d % 2, layer + 1)
        for e in first_edges if deep else ():
            @pl.when(corners[e][0])
            def _():
                edge_copy(e, e ^ 3, slot, raw).start()
        for d in first:
            @pl.when(sides[d][0])
            def _():
                face_copy(d, d ^ 1, slot, layers * rows, raw).start()
        u = split(value)
        if level == 0:
            for d in range(6):
                place_inner(lhs, u, d)
            lhs[6] = u.reshape(2, 2, 2, 2, 2, 16, 128).astype(bf16)
            for d in range(6):
                place_border(lhs, u, d, jnp.zeros((16, 8, 128), f32))
            fields = [lhs[d].reshape(512, 128) for d in range(weights.shape[0] // 256)]
            product = twice(jnp.concatenate(fields, axis=1), weights)
            inner[...] = chosen(product, m0[...]).reshape(inner.shape)
        for d in range(6):
            @pl.when(sides[d][0])
            def _():
                face_copy(d, d ^ 1, slot, layers * rows, raw).wait_send()
        if deep:
            for e in range(12):
                @pl.when(corners[e][0])
                def _():
                    edge_copy(e, e ^ 3, slot, raw).wait_send()
        for d in range(6):
            @pl.when(sides[d][0])
            def _():
                face_copy(d, d, slot, layers * rows, raw).wait_recv()
        if deep:
            for e in range(12):
                @pl.when(corners[e][0])
                def _():
                    edge_copy(e, e, slot, raw).wait_recv()
        near = [merged(lambda d: in_face[slot, d, :rows], level, dim, 1) for dim in range(3)]
        far, edges = None, None
        if deep:
            at = 0 if raw else rows
            far = [
                split_tiles(merged(lambda d: in_face[slot, d, at:at + rows], level, dim, 2)) for dim in range(3)
            ]
            edges = []
            for p, q in PAIRS:
                got = [
                    unpack_edge(in_edge[slot, e], level, p, q, sp, sq)
                    for e, (p_, q_, sp, sq) in enumerate(EDGES) if (p_, q_) == (p, q)
                ]
                got = [jnp.where(bit_is(q, 1), got[1], got[0]), jnp.where(bit_is(q, 1), got[3], got[2])]
                edges.append(split_tiles(jnp.where(bit_is(p, 1), got[1], got[0])))
        return u, near, far, edges

    def gathered(level, u, planes):
        if level == 0:
            for d in range(6):
                place_border(lhs, u, d, planes[d // 2])
            return [lhs[d].reshape(512, 128) for d in range(7)]
        fields = []
        for d in range(6):
            dim = d // 2
            field = shifted(own_tiles(u, level), (dim,) if level == 1 else (), dim, d % 2 == 0, planes[dim])
            fields.append(field.reshape(-1, 128))
        fields.append(u)
        if level == 2:
            fields = [jnp.concatenate([field, field], axis=0) for field in fields]
        return [field.astype(bf16) for field in fields]

    def with_halo(planes, weights):
        half = weights.shape[0] // 2
        material = own_tiles(m0[...], 0)
        for dim in range(3):
            upper = bit_is(dim, 1)
            both = [jnp.where(upper, planes[dim], 0.0), jnp.where(upper, 0.0, planes[dim])]
            both = jnp.concatenate([part.reshape(-1, 128) for part in both], axis=1).astype(bf16)
            at = 2 * dim * 128
            w = jnp.concatenate([weights[at:at + 256], weights[half + at:half + at + 256]], axis=0)
            product = jnp.dot(jnp.concatenate([both, both], axis=1), w, preferred_element_type=f32)
            rows = jnp.where(upper, outer(material, 0, dim, 1, 1), outer(material, 0, dim, 0, 1))
            term = chosen(product, rows.reshape(-1, 128)).reshape(2, 2, 2, 2, 8, 128)
            high, low = index_at(0, dim, 1, 1), index_at(0, dim, 0, 0)
            inner[high] = inner[high] + jnp.where(upper, term, 0.0)
            inner[low] = inner[low] + jnp.where(upper, 0.0, term)
        return inner[...].reshape(512, 128)

    def relaxed(level, value, u, planes):
        v, g, m = state[level]
        product = twice(jnp.concatenate(gathered(level, u, planes)[:6], axis=1), sweep_w)
        return (1.0 - WEIGHT) * value + g[...] + chosen(product[:ROWS[level]], m[...])

    def residual(level, u, planes):
        f = (f0, f1)[level]
        product = twice(jnp.concatenate(gathered(level, u, planes), axis=1), rest_w)
        return f[...] - chosen(product, state[level][2][...])

    def refilled(u):
        for d in range(6):
            place_inner(lhs, u, d)
        lhs[6] = u.reshape(2, 2, 2, 2, 2, 16, 128).astype(bf16)

    def double_step(level, step, fresh, last):
        v = state[level][0]
        halo_g, halo_m = halos[level]
        u, near, far, edges = exchange(level, step, True, sweep_w)
        planes = [split_tiles(tiles) for tiles in near]
        raw = jnp.concatenate([tiles.reshape(-1, 128) for tiles in near], axis=0)
        if fresh:
            halo_g[...] = raw
        rows = [halo_fields(u, level, dim, planes[dim], far[dim], edges) for dim in range(3)]
        rows = jnp.concatenate(rows, axis=0)
        count = rows.shape[0]
        if count % 16:
            rows = jnp.concatenate([rows, rows[:16 - count % 16]], axis=0)
        if level == 0:
            value = (1.0 - WEIGHT) * v[...] + g0[...] + with_halo(planes, sweep_w)
        else:
            value = relaxed(level, v[...], u, planes)
        product = twice(rows.astype(bf16), sweep_w)[:count]
        raw = (1.0 - WEIGHT) * raw + halo_g[...] + chosen(product, halo_m[...])
        planes = split(raw).reshape(3, -1, 8, 128)
        planes = [planes[dim] for dim in range(3)]
        u = split(value)
        if level == 0:
            refilled(u)
        if last == "sweep":
            v[...] = relaxed(level, value, u, planes)
            return None
        v[...] = value
        return residual(level, u, planes)

    def single_step(level, step, last):
        v = state[level][0]
        u, near, far, edges = exchange(level, step, False, sweep_w if last == "sweep" else rest_w)
        planes = [split_tiles(tiles) for tiles in near]
        if level == 0:
            return f0[...] - with_halo(planes, rest_w)
        if last == "sweep":
            v[...] = relaxed(level, v[...], u, planes)
            return None
        return residual(level, u, planes)

    def coarser(value):
        u = split(value)
        count = u.shape[0] // 8
        parts = [u[c * count:(c + 1) * count] for c in range(8)]
        if count == 8:
            parts = [jnp.concatenate([part, part], axis=0) for part in parts]
        return twice(jnp.concatenate(parts, axis=1).astype(bf16), restrict_w)[:count]

    def finer(value):
        u = split(value)
        count = u.shape[0]
        if count == 8:
            u = jnp.concatenate([u, u], axis=0)
        product = twice(u.astype(bf16), prolong_w)[:count]
        return jnp.concatenate([product[:, c * 128:(c + 1) * 128] for c in range(8)], axis=0)

    def wide(value):
        return jnp.concatenate([value, value], axis=0)

    for level in range(3):
        for d in range(6):
            @pl.when(sides[d][0])
            def _():
                mat_copy(d, d, level).wait_recv()
                mat_copy(d, d ^ 1, level).wait_send()
        planes = [
            merged(lambda d: in_mat[level, d, :FACE_ROWS[level]], level, dim, 1).reshape(-1, 128)
            for dim in range(3)
        ]
        halos[level][1][...] = jnp.concatenate(planes, axis=0) - 1.0

    @pl.loop(0, CYCLES)
    def _(cycle):
        @pl.when(cycle == 0)
        def _():
            f1[...] = coarser(double_step(0, 0, True, "residual"))

        @pl.when(cycle > 0)
        def _():
            double_step(0, 6, False, "sweep")
            f1[...] = coarser(single_step(0, 7, "residual"))
        base = 1 + 7 * cycle
        g1[...] = scaled_inverse(f1[...], m1[...])
        v1[...] = g1[...]
        f2 = coarser(double_step(1, base, True, "residual"))
        g2[...] = scaled_inverse(wide(f2), wide(m2[...]))[:8]
        v2[...] = g2[...]
        double_step(2, base + 1, True, "sweep")
        single_step(2, base + 2, "sweep")
        v1[...] = v1[...] + finer(v2[...])
        double_step(1, base + 3, False, "sweep")
        v0[...] = v0[...] + finer(v1[...])
        double_step(0, base + 4, False, "sweep")

    pieces = three(jnp.transpose(v0[...])[:MODES])
    back = []
    for half in range(2):
        columns = pl.ds(256 * half, 256)
        total = None
        for piece in pieces:
            part = jnp.dot(piece, order[:, columns], preferred_element_type=f32)
            total = part if total is None else total + part
        result[half] = total
        back.append(remote(
            result.at[half], out_ref.at[:, columns], send_block.at[4 + half], recv_block.at[4 + half], owner))
        back[half].start()
    for copy in back:
        copy.wait()


def per_device(sizes, right_side, diag_blocks, face_blocks, prolong, mats_fine, mats_mid, mats_coarse):
    def vmem(shape, dtype=f32):
        return pltpu.VMEM(shape, dtype)
    field = [vmem((512, 128))] * 4
    middle = [vmem((64, 128))] * 4
    coarse = [vmem((8, 128))] * 3
    result = pl.pallas_call(
        partial(kernel, sizes),
        out_shape=jax.ShapeDtypeStruct((MODES, 512), f32),
        in_specs=[pl.BlockSpec(memory_space=pltpu.VMEM)] * 7,
        out_specs=pl.BlockSpec(memory_space=pltpu.VMEM),
        scratch_shapes=[
            vmem((2 * 768, 256), bf16),
            vmem((2 * 896, 256), bf16),
            vmem((2 * 128, 256), bf16),
            vmem((2 * 1024, 128), bf16),
            vmem((2 * 128, 1024), bf16),
            vmem((512, 512), bf16),
            vmem((7, 2, 2, 2, 2, 2, 16, 128), bf16),
        ] + field + middle + coarse + [vmem((3 * n, 128)) for n in (128, 32, 8)] * 2 + [
            vmem((SLOTS, 6, 64, 128)),
            vmem((SLOTS, 6, 64, 128)),
            vmem((SLOTS, 12, 8, 128)),
            vmem((SLOTS, 12, 8, 128)),
            vmem((3, 6, 32, 128)),
            vmem((3, 6, 32, 128)),
        ] + [pltpu.SemaphoreType.DMA((SLOTS, n)) for n in (6, 6, 12, 12)] + [
            pltpu.SemaphoreType.DMA((3, 6)),
            pltpu.SemaphoreType.DMA((3, 6)),
            vmem((64, 512)),
            vmem((1, 512), jnp.int32),
            vmem((1, 64), jnp.int32),
            vmem((1, 8), jnp.int32),
            vmem((2, 64, 256)),
            pltpu.SemaphoreType.DMA((6,)),
            pltpu.SemaphoreType.DMA((6,)),
            vmem((2, 2, 2, 2, 2, 2, 8, 128)),
        ],
        compiler_params=pltpu.CompilerParams(collective_id=0, has_side_effects=True),
        name="cycles",
    )(
        right_side[0, 0, 0], diag_blocks, face_blocks, prolong,
        mats_fine.reshape(1, -1), mats_mid.reshape(1, -1), mats_coarse.reshape(1, -1),
    )
    return result[None, None, None]


def solution(mesh):
    placed = (
        P("gx", "gy", "gz", None, None),
        P(),
        P(),
        P(),
        P("gx", "gy", "gz", None),
        P("gx", "gy", "gz", None),
        P("gx", "gy", "gz", None),
    )
    sizes = tuple(mesh.shape[axis] for axis in AXES)
    return jax.shard_map(
        partial(per_device, sizes),
        mesh=mesh,
        in_specs=placed,
        out_specs=P("gx", "gy", "gz", None, None),
        check_vma=False,
    )
```

```python
from functools import partial

import jax
import jax.numpy as jnp
from jax import lax
from jax.experimental import pallas as pl
from jax.experimental.pallas import tpu as pltpu
from jax.sharding import PartitionSpec as P

MODES = 64
MATERIALS = 4
SWEEPS = 2
COARSE_SWEEPS = 4
CYCLES = 2
ROWS = (512, 64, 8)
TILE_DIMS = ((2, 2, 2, 2, 2, 2), (2, 2, 2), ())
FACE_ROWS = (32, 8, 8)
AXES = ("gx", "gy", "gz")
WEIGHT = 0.7
SCALE = 0.6
SUB = (4, 2, 1)
f32 = jnp.float32
bf16 = jnp.bfloat16
highest = lax.Precision.HIGHEST


def lanes(rows):
    return lax.broadcasted_iota(jnp.int32, (rows, 128), 1)


def swap_halves(x):
    return pltpu.roll(x, 64, axis=1)


def split(x):
    high = x.astype(bf16).astype(f32)
    return jnp.where(lanes(x.shape[0]) < 64, high, x - high)


def bit_is(dim, value):
    sub = lax.broadcasted_iota(jnp.int32, (8, 128), 0)
    return (jnp.right_shift(sub, 2 - dim) & 1) == value


def roll_sub(x, amount):
    shape = x.shape
    return pltpu.roll(x.reshape(-1, 8, 128), (-amount) % 8, axis=1).reshape(shape)


def pair(weights):
    high = weights.astype(bf16)
    return high, (weights - high.astype(f32)).astype(bf16)


def chosen(product, material):
    rows = product.shape[0]
    half = jnp.where(lanes(rows) < 64, 0.0, 1.0)
    offset = material - half
    kept = jnp.where(offset == 0.0, product[:, :128], jnp.where(offset == 2.0, product[:, 128:], 0.0))
    return kept + swap_halves(kept)


def twice(x, w_ref):
    return jnp.dot(jnp.concatenate([x, x], axis=1), w_ref[...], preferred_element_type=f32)


def three(x):
    a = x.astype(bf16)
    rest = x - a.astype(f32)
    b = rest.astype(bf16)
    return a, b, (rest - b.astype(f32)).astype(bf16)


def element_of_row(row):
    def bit(n):
        return jnp.right_shift(row, n) & 1
    x = bit(8) + 2 * bit(5) + 4 * bit(2)
    y = bit(7) + 2 * bit(4) + 4 * bit(1)
    z = bit(6) + 2 * bit(3) + 4 * bit(0)
    return x * 64 + y * 8 + z


def middle_of_row(row):
    def bit(n):
        return jnp.right_shift(row, n) & 1
    x = bit(5) + 2 * bit(2)
    y = bit(4) + 2 * bit(1)
    z = bit(3) + 2 * bit(0)
    return x * 16 + y * 4 + z


def spread_materials(mats, rows, place):
    row = lax.broadcasted_iota(jnp.int32, (rows, rows), 0)
    col = lax.broadcasted_iota(jnp.int32, (rows, rows), 1)
    kept = jnp.where(place(row) == col, jnp.broadcast_to(mats.astype(f32), (rows, rows)), 0.0)
    return jnp.broadcast_to(jnp.sum(kept, axis=1, keepdims=True), (rows, 128))


def invert(blocks):
    row_id = lax.broadcasted_iota(jnp.int32, blocks.shape, 1)
    lane_id = lax.broadcasted_iota(jnp.int32, blocks.shape, 2)
    for k in range(MODES):
        pivot = 1.0 / blocks[:, k:k + 1, k:k + 1]
        at_lane = lane_id == k
        row = jnp.where(at_lane[:, :1, :], 1.0, blocks[:, k:k + 1, :]) * pivot
        column = blocks[:, :, k:k + 1]
        rest = jnp.where(at_lane, 0.0, blocks) - column * row
        blocks = jnp.where(row_id == k, row, rest)
    return blocks


def prepare(diag_ref, face_ref, prolong_ref, sweep_w, rest_w, inv_w, restrict_w, prolong_w):
    inverse = invert(diag_ref[...])

    def side(parts):
        return jnp.concatenate(parts, axis=1)

    def store(ref, at, w):
        high, low = pair(w)
        half = ref.shape[0] // 2
        ref[at:at + 128] = jnp.concatenate([high, high], axis=0)
        ref[half + at:half + at + 128] = jnp.concatenate([low, low], axis=0)
    store(inv_w, 0, WEIGHT * side([inverse[m] for m in range(MATERIALS)]))
    store(rest_w, 6 * 128, side([diag_ref[m] for m in range(MATERIALS)]))
    for d in range(6):
        turned = [jnp.transpose(face_ref[d, m]) for m in range(MATERIALS)]
        store(rest_w, d * 128, side(turned))
        mixed = [
            jnp.dot(turned[m], inverse[m], precision=highest, preferred_element_type=f32)
            for m in range(MATERIALS)
        ]
        store(sweep_w, d * 128, -WEIGHT * side(mixed))
    for c in range(8):
        block = SCALE * prolong_ref[c]
        store(restrict_w, c * 128, side([block, block]))
        back = jnp.transpose(prolong_ref[c])
        high, low = pair(side([back, back]))
        columns = slice(c * 128, c * 128 + 128)
        prolong_w[0:128, columns] = jnp.concatenate([high, high], axis=0)
        prolong_w[128:256, columns] = jnp.concatenate([low, low], axis=0)


def index_at(level, dim, *bits):
    at = [slice(None)] * len(TILE_DIMS[level])
    for i, b in enumerate(bits):
        at[3 * i + dim] = b
    return tuple(at)


def depth(level):
    return 2 - level


PAIRS = ((0, 1), (0, 2), (1, 2))
EDGES = tuple((p, q, sp, sq) for p, q in PAIRS for sp in (0, 1) for sq in (0, 1))
SLOTS = 3


def own_tiles(value, level):
    return value.reshape(TILE_DIMS[level] + (8, 128))


def outer(tiles, level, dim, upper, layer):
    bits = [upper] * depth(level)
    if layer == 2 and bits:
        bits[0] = 1 - upper
    return tiles[index_at(level, dim, *bits)].reshape(-1, 8, 128)


def toward(dim, upper):
    return SUB[dim] if upper else -SUB[dim]


def two_halves(packed):
    other = swap_halves(packed.reshape(-1, 128)).reshape(packed.shape)
    low_lanes = lanes(8) < 64
    return jnp.concatenate([jnp.where(low_lanes, packed, other), jnp.where(low_lanes, other, packed)], axis=0)


def pack_face(tiles, level, dim, upper, layer):
    tiles = outer(tiles, level, dim, upper, layer)
    half = tiles.shape[0] // 2
    packed = jnp.where(bit_is(dim, 1 - upper), roll_sub(tiles[:half], toward(dim, upper)), tiles[half:])
    half = half // 2
    return jnp.where(lanes(8) < 64, packed[:half], packed[half:]).reshape(-1, 128)


def unpack_face(packed, level, dim, upper, layer):
    packed = packed.reshape(-1, 8, 128)
    if level == 2:
        return packed if layer == 2 else roll_sub(packed, -toward(dim, upper))
    both = two_halves(packed)
    return jnp.concatenate([both, roll_sub(both, -toward(dim, upper))], axis=0)


def pack_edge(tiles, level, p, q, sp, sq):
    at = list(index_at(level, p, *([sp] * depth(level))))
    for i, b in enumerate(index_at(level, q, *([sq] * depth(level)))):
        at[i] = b if at[i] == slice(None) else at[i]
    tiles = tiles[tuple(at)].reshape(-1, 8, 128)
    half = tiles.shape[0] // 2
    if level == 0:
        moved = roll_sub(tiles[:half], toward(p, sp) + toward(q, sq))
        tiles = jnp.where(bit_is(p, 1 - sp), moved, roll_sub(tiles[half:], toward(q, sq)))
    else:
        tiles = roll_sub(tiles, toward(p, sp) + toward(q, sq))
    return jnp.where(lanes(8) < 64, tiles[0], tiles[1])


def unpack_edge(packed, level, p, q, sp, sq):
    packed = packed.reshape(1, 8, 128)
    if level == 2:
        return roll_sub(packed, -toward(p, sp) - toward(q, sq))
    both = two_halves(packed)
    if level == 1:
        return both
    return jnp.concatenate([both, roll_sub(both, -toward(p, sp))], axis=0)


def split_tiles(tiles):
    return split(tiles.reshape(-1, 128)).reshape(tiles.shape)


def border(tiles, halo, dim, up):
    rolled = roll_sub(tiles, SUB[dim] if up else -SUB[dim])
    return jnp.where(bit_is(dim, 0 if up else 1), rolled, halo.reshape(tiles.shape))


def take(tiles, axis, bit):
    at = [slice(None)] * tiles.ndim
    at[axis] = bit
    return tiles[tuple(at)]


def shifted(tiles, axes, dim, up, halo):
    if not axes:
        return border(tiles, halo, dim, up)
    near, far = (0, 1) if up else (1, 0)

    def ordered(at_near, at_far, axis):
        return jnp.stack([at_near, at_far] if up else [at_far, at_near], axis=axis)
    if len(axes) == 1:
        return ordered(take(tiles, axes[0], far), border(take(tiles, axes[0], near), halo, dim, up), axes[0])
    kept = take(tiles, axes[0], near)
    deeper = axes[1] - 1
    end = border(take(kept, deeper, near), halo, dim, up)
    return ordered(take(tiles, axes[0], far), ordered(take(kept, deeper, far), end, deeper), axes[0])


def place_inner(lhs, u, d):
    dim, up = d // 2, d % 2 == 0
    tiles = own_tiles(u, 0)
    near, far = (0, 1) if up else (1, 0)

    def put(where, value):
        shape = value.shape[:-3] + (16, 128)
        lhs[(d,) + where] = value.reshape(shape).astype(bf16)
    put(index_at(0, dim, near)[:5], tiles[index_at(0, dim, far)])
    if dim < 2:
        put(index_at(0, dim, far, near)[:5], tiles[index_at(0, dim, near, far)])


def place_border(lhs, u, d, halo):
    dim, up = d // 2, d % 2 == 0
    tiles = own_tiles(u, 0)
    near, far = (0, 1) if up else (1, 0)
    edge = border(tiles[index_at(0, dim, near, near)], halo, dim, up)
    if dim < 2:
        lhs[(d,) + index_at(0, dim, far, far)[:5]] = edge.reshape(edge.shape[:-3] + (16, 128)).astype(bf16)
    else:
        inner = tiles[index_at(0, dim, near, far)]
        both = [inner, edge] if up else [edge, inner]
        both = jnp.concatenate(both, axis=-2)
        lhs[d, :, :, far] = both.astype(bf16)


def halo_fields(u, level, dim, near, far, edges):
    tiles = own_tiles(u, level)
    others = [i for i in range(3) if i != dim]
    bits = near.reshape((2,) * (2 * depth(level)) + (8, 128))
    fields = []
    for d in range(6):
        along, up = d // 2, d % 2 == 0
        if along == dim:
            own = outer(tiles, level, dim, 0 if up else 1, 1)
            field = jnp.where(bit_is(dim, 1 if up else 0), far, own)
        else:
            axes = [others.index(along) + 2 * i for i in range(depth(level))]
            field = shifted(bits, axes, along, up, edges[PAIRS.index((min(dim, along), max(dim, along)))])
        fields.append(field.reshape(-1, 128))
    return jnp.concatenate(fields, axis=1)


def kernel(
    sizes, rhs_ref, diag_ref, face_ref, prolong_ref, fine_ref, mid_ref, coarse_ref, out_ref,
    sweep_w, rest_w, inv_w, restrict_w, prolong_w, order, lhs,
    v0, f0, g0, m0, v1, f1, g1, m1, v2, g2, m2,
    halo_g0, halo_g1, halo_g2, halo_m0, halo_m1, halo_m2,
    out_face, in_face, out_edge, in_edge, out_mat, in_mat,
    send_face, recv_face, send_edge, recv_edge, send_mat, recv_mat,
    rhs_box, fine_box, mid_box, coarse_box, result, send_block, recv_block, inner,
):
    home = tuple(lax.axis_index(axis) for axis in AXES)
    run = sizes[1] // sizes[2]
    shift = run // 2

    def holder(x, y, z):
        along = lax.rem(y + shift + sizes[1], sizes[1])
        return x, z * run + lax.rem(along, run), along // run
    worker = holder(*home)
    along = home[2] * run + lax.rem(home[1], run)
    place = [home[0], lax.rem(along - shift + sizes[1], sizes[1]), home[1] // run]
    owner = tuple(place)
    able = [((place[i] > 0), (place[i] < sizes[i] - 1)) for i in range(3)]

    def device(*moves):
        there = list(place)
        for dim, upper in moves:
            there[dim] = there[dim] + (1 if upper else -1)
        return holder(*there)
    sides = [(able[dim][upper], device((dim, upper))) for dim in range(3) for upper in (1, 0)]
    corners = [(able[p][sp] & able[q][sq], device((p, sp), (q, sq))) for p, q, sp, sq in EDGES]
    first = (2, 3, 4, 5, 0, 1)
    first_edges = (8, 9, 10, 11, 0, 1, 2, 3, 4, 5, 6, 7)

    barrier = pltpu.get_barrier_semaphore()
    for exists, there in sides + corners:
        @pl.when(exists)
        def _():
            pl.semaphore_signal(barrier, inc=1, device_id=there, device_id_type=pl.DeviceIdType.MESH)
    for there in (worker, owner):
        pl.semaphore_signal(barrier, inc=1, device_id=there, device_id_type=pl.DeviceIdType.MESH)
    pl.semaphore_wait(barrier, 2 + sum(exists.astype(jnp.int32) for exists, there in sides + corners))

    def remote(src, dst, send, recv, there):
        return pltpu.make_async_remote_copy(
            src_ref=src, dst_ref=dst, send_sem=send, recv_sem=recv,
            device_id=there, device_id_type=pl.DeviceIdType.MESH)
    moved = [
        remote(src, dst, send_block.at[i], recv_block.at[i], worker)
        for i, (src, dst) in enumerate((
            (fine_ref, fine_box), (mid_ref, mid_box), (coarse_ref, coarse_box), (rhs_ref, rhs_box)))
    ]
    for copy in moved:
        copy.start()
    for d, (exists, there) in enumerate(sides):
        @pl.when(jnp.logical_not(exists))
        def _():
            in_face[:, d] = jnp.zeros((SLOTS, 64, 128), f32)
            in_mat[:, d] = jnp.zeros((3, 32, 128), f32)
    for e, (exists, there) in enumerate(corners):
        @pl.when(jnp.logical_not(exists))
        def _():
            in_edge[:, e] = jnp.zeros((SLOTS, 8, 128), f32)

    def face_copy(d, land, slot, rows, raw):
        rows = pl.ds(0, rows)
        return remote(
            out_face.at[slot, 0 if raw else d, rows], in_face.at[slot, land, rows],
            send_face.at[slot, d], recv_face.at[slot, land], sides[d][1])

    def edge_copy(e, land, slot, raw):
        src = out_face.at[slot, 0, pl.ds(0, 8)] if raw else out_edge.at[slot, e]
        return remote(src, in_edge.at[slot, land], send_edge.at[slot, e], recv_edge.at[slot, land], corners[e][1])

    def mat_copy(d, land, level):
        rows = pl.ds(0, FACE_ROWS[level])
        return remote(
            out_mat.at[level, d, rows], in_mat.at[level, land, rows],
            send_mat.at[level, d], recv_mat.at[level, land], sides[d][1])

    row = lax.broadcasted_iota(jnp.int32, (512, 512), 0)
    col = lax.broadcasted_iota(jnp.int32, (512, 512), 1)
    order[...] = jnp.where(element_of_row(row) == col, 1.0, 0.0).astype(bf16)
    prepare(diag_ref, face_ref, prolong_ref, sweep_w, rest_w, inv_w, restrict_w, prolong_w)
    for copy in moved[:3]:
        copy.wait()
    m0[...] = lax.dot_general(
        order[...], jnp.broadcast_to(fine_box[...].astype(f32), (128, 512)).astype(bf16),
        (((1,), (1,)), ((), ())), preferred_element_type=f32)
    m1[...] = spread_materials(mid_box[...], 64, middle_of_row)
    m2[...] = spread_materials(coarse_box[...], 8, lambda r: r)
    for level, m in enumerate((m0, m1, m2)):
        tiles = own_tiles(m[...] + 1.0, level)
        for d in first:
            packed = tiles if level == 2 else pack_face(tiles, level, d // 2, 1 - d % 2, 1)
            out_mat[level, d, :FACE_ROWS[level]] = packed
    for level in range(3):
        for d in first:
            @pl.when(sides[d][0])
            def _():
                mat_copy(d, d ^ 1, level).start()

    moved[3].wait()
    source = jnp.concatenate([rhs_box[...], rhs_box[...]], axis=0)
    total = None
    for piece in three(source):
        part = lax.dot_general(order[...], piece, (((1,), (1,)), ((), ())), preferred_element_type=f32)
        total = part if total is None else total + part
    f0[...] = total

    def scaled_inverse(value, material):
        return chosen(twice(split(value).astype(bf16), inv_w), material)

    g0[...] = scaled_inverse(f0[...], m0[...])
    v0[...] = g0[...]
    state = ((v0, g0, m0), (v1, g1, m1), (v2, g2, m2))
    halos = ((halo_g0, halo_m0), (halo_g1, halo_m1), (halo_g2, halo_m2))

    def merged(read, level, dim, layer):
        above = unpack_face(read(2 * dim), level, dim, 1, layer)
        below = unpack_face(read(2 * dim + 1), level, dim, 0, layer)
        return jnp.where(bit_is(dim, 1), above, below)

    def exchange(level, step, deep, weights):
        slot = lax.rem(step, SLOTS)
        rows = FACE_ROWS[level]
        raw = level == 2
        layers = 2 if deep and not raw else 1
        value = state[level][0][...]
        tiles = own_tiles(value, level)
        if raw:
            out_face[slot, 0, :8] = value
        if not raw:
            for e in first_edges if deep else ():
                out_edge[slot, e] = pack_edge(tiles, level, *EDGES[e])
            for d in first:
                for layer in range(layers):
                    out_face[slot, d, layer * rows:layer * rows + rows] = pack_face(
                        tiles, level, d // 2, 1 - d % 2, layer + 1)
        for e in first_edges if deep else ():
            @pl.when(corners[e][0])
            def _():
                edge_copy(e, e ^ 3, slot, raw).start()
        for d in first:
            @pl.when(sides[d][0])
            def _():
                face_copy(d, d ^ 1, slot, layers * rows, raw).start()
        u = split(value)
        if level == 0:
            for d in range(6):
                place_inner(lhs, u, d)
            lhs[6] = u.reshape(2, 2, 2, 2, 2, 16, 128).astype(bf16)
            for d in range(6):
                place_border(lhs, u, d, jnp.zeros((16, 8, 128), f32))
            fields = [lhs[d].reshape(512, 128) for d in range(weights.shape[0] // 256)]
            product = twice(jnp.concatenate(fields, axis=1), weights)
            inner[...] = chosen(product, m0[...]).reshape(inner.shape)
        for d in range(6):
            @pl.when(sides[d][0])
            def _():
                face_copy(d, d ^ 1, slot, layers * rows, raw).wait_send()
        if deep:
            for e in range(12):
                @pl.when(corners[e][0])
                def _():
                    edge_copy(e, e ^ 3, slot, raw).wait_send()
        for d in range(6):
            @pl.when(sides[d][0])
            def _():
                face_copy(d, d, slot, layers * rows, raw).wait_recv()
        if deep:
            for e in range(12):
                @pl.when(corners[e][0])
                def _():
                    edge_copy(e, e, slot, raw).wait_recv()
        near = [merged(lambda d: in_face[slot, d, :rows], level, dim, 1) for dim in range(3)]
        far, edges = None, None
        if deep:
            at = 0 if raw else rows
            far = [
                split_tiles(merged(lambda d: in_face[slot, d, at:at + rows], level, dim, 2)) for dim in range(3)
            ]
            edges = []
            for p, q in PAIRS:
                got = [
                    unpack_edge(in_edge[slot, e], level, p, q, sp, sq)
                    for e, (p_, q_, sp, sq) in enumerate(EDGES) if (p_, q_) == (p, q)
                ]
                got = [jnp.where(bit_is(q, 1), got[1], got[0]), jnp.where(bit_is(q, 1), got[3], got[2])]
                edges.append(split_tiles(jnp.where(bit_is(p, 1), got[1], got[0])))
        return u, near, far, edges

    def gathered(level, u, planes):
        if level == 0:
            for d in range(6):
                place_border(lhs, u, d, planes[d // 2])
            return [lhs[d].reshape(512, 128) for d in range(7)]
        fields = []
        for d in range(6):
            dim = d // 2
            field = shifted(own_tiles(u, level), (dim,) if level == 1 else (), dim, d % 2 == 0, planes[dim])
            fields.append(field.reshape(-1, 128))
        fields.append(u)
        if level == 2:
            fields = [jnp.concatenate([field, field], axis=0) for field in fields]
        return [field.astype(bf16) for field in fields]

    def with_halo(planes, weights):
        half = weights.shape[0] // 2
        material = own_tiles(m0[...], 0)
        for dim in range(3):
            upper = bit_is(dim, 1)
            both = [jnp.where(upper, planes[dim], 0.0), jnp.where(upper, 0.0, planes[dim])]
            both = jnp.concatenate([part.reshape(-1, 128) for part in both], axis=1).astype(bf16)
            at = 2 * dim * 128
            w = jnp.concatenate([weights[at:at + 256], weights[half + at:half + at + 256]], axis=0)
            product = jnp.dot(jnp.concatenate([both, both], axis=1), w, preferred_element_type=f32)
            rows = jnp.where(upper, outer(material, 0, dim, 1, 1), outer(material, 0, dim, 0, 1))
            term = chosen(product, rows.reshape(-1, 128)).reshape(2, 2, 2, 2, 8, 128)
            high, low = index_at(0, dim, 1, 1), index_at(0, dim, 0, 0)
            inner[high] = inner[high] + jnp.where(upper, term, 0.0)
            inner[low] = inner[low] + jnp.where(upper, 0.0, term)
        return inner[...].reshape(512, 128)

    def relaxed(level, value, u, planes):
        v, g, m = state[level]
        product = twice(jnp.concatenate(gathered(level, u, planes)[:6], axis=1), sweep_w)
        return (1.0 - WEIGHT) * value + g[...] + chosen(product[:ROWS[level]], m[...])

    def residual(level, u, planes):
        f = (f0, f1)[level]
        product = twice(jnp.concatenate(gathered(level, u, planes), axis=1), rest_w)
        return f[...] - chosen(product, state[level][2][...])

    def refilled(u):
        for d in range(6):
            place_inner(lhs, u, d)
        lhs[6] = u.reshape(2, 2, 2, 2, 2, 16, 128).astype(bf16)

    def double_step(level, step, fresh, last):
        v = state[level][0]
        halo_g, halo_m = halos[level]
        u, near, far, edges = exchange(level, step, True, sweep_w)
        planes = [split_tiles(tiles) for tiles in near]
        raw = jnp.concatenate([tiles.reshape(-1, 128) for tiles in near], axis=0)
        if fresh:
            halo_g[...] = raw
        rows = [halo_fields(u, level, dim, planes[dim], far[dim], edges) for dim in range(3)]
        rows = jnp.concatenate(rows, axis=0)
        count = rows.shape[0]
        if count % 16:
            rows = jnp.concatenate([rows, rows[:16 - count % 16]], axis=0)
        if level == 0:
            value = (1.0 - WEIGHT) * v[...] + g0[...] + with_halo(planes, sweep_w)
        else:
            value = relaxed(level, v[...], u, planes)
        product = twice(rows.astype(bf16), sweep_w)[:count]
        raw = (1.0 - WEIGHT) * raw + halo_g[...] + chosen(product, halo_m[...])
        planes = split(raw).reshape(3, -1, 8, 128)
        planes = [planes[dim] for dim in range(3)]
        u = split(value)
        if level == 0:
            refilled(u)
        if last == "sweep":
            v[...] = relaxed(level, value, u, planes)
            return None
        v[...] = value
        return residual(level, u, planes)

    def single_step(level, step, last):
        v = state[level][0]
        u, near, far, edges = exchange(level, step, False, sweep_w if last == "sweep" else rest_w)
        planes = [split_tiles(tiles) for tiles in near]
        if level == 0:
            return f0[...] - with_halo(planes, rest_w)
        if last == "sweep":
            v[...] = relaxed(level, v[...], u, planes)
            return None
        return residual(level, u, planes)

    def coarser(value):
        u = split(value)
        count = u.shape[0] // 8
        parts = [u[c * count:(c + 1) * count] for c in range(8)]
        if count == 8:
            parts = [jnp.concatenate([part, part], axis=0) for part in parts]
        return twice(jnp.concatenate(parts, axis=1).astype(bf16), restrict_w)[:count]

    def finer(value):
        u = split(value)
        count = u.shape[0]
        if count == 8:
            u = jnp.concatenate([u, u], axis=0)
        product = twice(u.astype(bf16), prolong_w)[:count]
        return jnp.concatenate([product[:, c * 128:(c + 1) * 128] for c in range(8)], axis=0)

    def wide(value):
        return jnp.concatenate([value, value], axis=0)

    for level in range(3):
        for d in range(6):
            @pl.when(sides[d][0])
            def _():
                mat_copy(d, d, level).wait_recv()
                mat_copy(d, d ^ 1, level).wait_send()
        planes = [
            merged(lambda d: in_mat[level, d, :FACE_ROWS[level]], level, dim, 1).reshape(-1, 128)
            for dim in range(3)
        ]
        halos[level][1][...] = jnp.concatenate(planes, axis=0) - 1.0

    @pl.loop(0, CYCLES)
    def _(cycle):
        @pl.when(cycle == 0)
        def _():
            f1[...] = coarser(double_step(0, 0, True, "residual"))

        @pl.when(cycle > 0)
        def _():
            double_step(0, 6, False, "sweep")
            f1[...] = coarser(single_step(0, 7, "residual"))
        base = 1 + 7 * cycle
        g1[...] = scaled_inverse(f1[...], m1[...])
        v1[...] = g1[...]
        f2 = coarser(double_step(1, base, True, "residual"))
        g2[...] = scaled_inverse(wide(f2), wide(m2[...]))[:8]
        v2[...] = g2[...]
        double_step(2, base + 1, True, "sweep")
        single_step(2, base + 2, "sweep")
        v1[...] = v1[...] + finer(v2[...])
        double_step(1, base + 3, False, "sweep")
        v0[...] = v0[...] + finer(v1[...])
        double_step(0, base + 4, False, "sweep")

    pieces = three(jnp.transpose(v0[...])[:MODES])
    back = []
    for half in range(2):
        columns = pl.ds(256 * half, 256)
        total = None
        for piece in pieces:
            part = jnp.dot(piece, order[:, columns], preferred_element_type=f32)
            total = part if total is None else total + part
        result[half] = total
        back.append(remote(
            result.at[half], out_ref.at[:, columns], send_block.at[4 + half], recv_block.at[4 + half], owner))
        back[half].start()
    for copy in back:
        copy.wait()


def per_device(sizes, right_side, diag_blocks, face_blocks, prolong, mats_fine, mats_mid, mats_coarse):
    def vmem(shape, dtype=f32):
        return pltpu.VMEM(shape, dtype)
    field = [vmem((512, 128))] * 4
    middle = [vmem((64, 128))] * 4
    coarse = [vmem((8, 128))] * 3
    result = pl.pallas_call(
        partial(kernel, sizes),
        out_shape=jax.ShapeDtypeStruct((MODES, 512), f32),
        in_specs=[pl.BlockSpec(memory_space=pl.ANY)] + [pl.BlockSpec(memory_space=pltpu.VMEM)] * 6,
        out_specs=pl.BlockSpec(memory_space=pltpu.VMEM),
        scratch_shapes=[
            vmem((2 * 768, 256), bf16),
            vmem((2 * 896, 256), bf16),
            vmem((2 * 128, 256), bf16),
            vmem((2 * 1024, 128), bf16),
            vmem((2 * 128, 1024), bf16),
            vmem((512, 512), bf16),
            vmem((7, 2, 2, 2, 2, 2, 16, 128), bf16),
        ] + field + middle + coarse + [vmem((3 * n, 128)) for n in (128, 32, 8)] * 2 + [
            vmem((SLOTS, 6, 64, 128)),
            vmem((SLOTS, 6, 64, 128)),
            vmem((SLOTS, 12, 8, 128)),
            vmem((SLOTS, 12, 8, 128)),
            vmem((3, 6, 32, 128)),
            vmem((3, 6, 32, 128)),
        ] + [pltpu.SemaphoreType.DMA((SLOTS, n)) for n in (6, 6, 12, 12)] + [
            pltpu.SemaphoreType.DMA((3, 6)),
            pltpu.SemaphoreType.DMA((3, 6)),
            vmem((64, 512)),
            vmem((1, 512), jnp.int32),
            vmem((1, 64), jnp.int32),
            vmem((1, 8), jnp.int32),
            vmem((2, 64, 256)),
            pltpu.SemaphoreType.DMA((6,)),
            pltpu.SemaphoreType.DMA((6,)),
            vmem((2, 2, 2, 2, 2, 2, 8, 128)),
        ],
        compiler_params=pltpu.CompilerParams(collective_id=0, has_side_effects=True),
        name="cycles",
    )(
        right_side[0, 0, 0], diag_blocks, face_blocks, prolong,
        mats_fine.reshape(1, -1), mats_mid.reshape(1, -1), mats_coarse.reshape(1, -1),
    )
    return result[None, None, None]


def solution(mesh):
    placed = (
        P("gx", "gy", "gz", None, None),
        P(),
        P(),
        P(),
        P("gx", "gy", "gz", None),
        P("gx", "gy", "gz", None),
        P("gx", "gy", "gz", None),
    )
    sizes = tuple(mesh.shape[axis] for axis in AXES)
    return jax.shard_map(
        partial(per_device, sizes),
        mesh=mesh,
        in_specs=placed,
        out_specs=P("gx", "gy", "gz", None, None),
        check_vma=False,
    )
```
